512 devices in a mesh: blk: 8 (over y, core), tiles: 64 (over z, x).
Axes of the slice: x: 4, y: 4, z: 16, core: 2. Of those that a mesh axis runs over, the one named last changes fastest.
Arguments:
- tensor_tiles: bfloat16 [8, 128, 64, 4096], P('blk', 'tiles'), may hold values from -6 to 6
- tile_iblock: int32 [8, 128], P('blk', 'tiles'), may hold values from 0 to 7
- tile_jslot: int32 [8, 128], P('blk', 'tiles'), may hold values from 0 to 1, as said below
- tile_kslot: int32 [8, 128], P('blk', 'tiles'), may hold values from 0 to 1, as said below
- block_jlist: int32 [8, 128], P('blk', 'tiles'), may hold values from 0 to 255, as said below
- block_klist: int32 [8, 128], P('blk', 'tiles'), may hold values from 0 to 63, as said below
- factor_b: bfloat16 [256, 64, 512], P(None, 'tiles'), may hold values from -0.5 to 0.5
- factor_c: bfloat16 [64, 64, 512], P(None, 'tiles'), may hold values from -0.75 to 0.75
Outputs:
- mttkrp: float32 [32768, 512], P(('blk', 'tiles'))
The draws below stay inside these ranges and needn't reach their ends.
Inputs may be any that keep to these rules, and one draw needn't show every extreme that they name: `block_jlist`: the 2 entries of one device's list are distinct. `block_klist`: the 2 entries of one device's list are distinct. `tile_jslot`: one device's tiles use between 1 and 2 distinct positions, and all 2 on some device. `tile_kslot`: one device's tiles use between 1 and 2 distinct positions, and all 2 on some device.
All inputs are finite; a program needn't handle non-finite values.
Results may differ from the reference program's by a relative error of at most 0.011.
Values may be sent and summed in bfloat16 or wider, within the bound.
A program may use at most 64 MiB of HBM per device.

```python
import jax
import jax.numpy as jnp
from jax import lax

TI = 64
TJ = 64
TK = 64
RANK = 512
TPD = 2
DIST = 2
JB = 256
KB = 64
TILE_COLS = 128
N_BLK = 8
N_TILES = 64


def slot_positions(key):
    devices = N_BLK * N_TILES
    key_count, key_top, key_fill, key_order = jax.random.split(key, 4)
    counts = jax.random.randint(key_count, (devices,), 1, DIST + 1)
    chosen = jax.random.randint(key_top, (), 0, devices)
    counts = jnp.where(jnp.arange(devices) == chosen, DIST, counts)
    position = jnp.arange(TPD)
    filler = jax.random.randint(key_fill, (devices, TPD), 0, 65536) % counts[:, None]
    slots = jnp.where(position[None, :] < counts[:, None], position[None, :], filler)
    scores = jax.random.randint(key_order, (devices, TPD), 0, 65536) * TPD + position[None, :]
    order = jnp.argsort(scores, axis=1)
    slots = jnp.take_along_axis(slots, order, axis=1)
    return slots.reshape(N_BLK, N_TILES * TPD).astype(jnp.int32)


def distinct_lists(key, total):
    devices = N_BLK * N_TILES
    scores = jax.random.randint(key, (devices, total), 0, 65536) * total + jnp.arange(total)[None, :]
    order = jnp.argsort(scores, axis=1)[:, :DIST]
    return order.reshape(N_BLK, N_TILES * DIST).astype(jnp.int32)


def draw_tile_jslot(key, part):
    return slot_positions(jax.random.fold_in(key, 11))


def draw_tile_kslot(key, part):
    return slot_positions(jax.random.fold_in(key, 23))


def draw_block_jlist(key, part):
    return distinct_lists(jax.random.fold_in(key, 37), JB)


def draw_block_klist(key, part):
    return distinct_lists(jax.random.fold_in(key, 41), KB)


def plant(entries, key, smallest, high):
    extent = entries.shape
    place = [jax.random.randint(jax.random.fold_in(key, axis), (), 0, extent[axis]) for axis in range(len(extent))]
    entries = entries.at[tuple(place)].set(smallest)
    longest = extent.index(max(extent))
    place[longest] = (place[longest] + 1) % extent[longest]
    return entries.at[tuple(place)].set(high)


def level_of(key, dims, shards, least, largest):
    def one(dim, parts):
        steps = jax.random.uniform(jax.random.fold_in(jax.random.fold_in(key, 6), dim), (parts,), jnp.float32, least / len(shards), largest / len(shards))
        return jnp.repeat(jnp.exp(steps), dims[dim] // parts).reshape((-1,) + (1,) * (len(dims) - dim - 1))

    gain = one(*shards[0])
    for cut in shards[1:]:
        gain = gain * one(*cut)
    return gain


def noise(key, extent, width, most, cuts=(), kind=jnp.bfloat16):
    factor_of = level_of(key, extent, cuts, -0.22, 0.18) if cuts else 1.0
    values = jax.random.normal(key, extent, jnp.float32) * width * factor_of
    return jnp.minimum(jnp.maximum(values, -most), most).astype(kind)


def setup_inputs(seed: int = 0) -> dict:
    keys = jax.random.split(jax.random.key(seed), 9)
    return {
        "tensor_tiles": noise(keys[0], (N_BLK, TILE_COLS, TI, TJ * TK), 1.0, 6.0, ((0, 8), (1, 64))),
        "tile_iblock": plant(jax.random.randint(keys[1], (N_BLK, TILE_COLS), 0, N_BLK), jax.random.fold_in(keys[1], 1), 0, N_BLK - 1).astype(jnp.int32),
        "tile_jslot": draw_tile_jslot(jax.random.fold_in(keys[8], 71), 0),
        "tile_kslot": draw_tile_kslot(jax.random.fold_in(keys[8], 71), 0),
        "block_jlist": draw_block_jlist(jax.random.fold_in(keys[8], 71), 0),
        "block_klist": draw_block_klist(jax.random.fold_in(keys[8], 71), 0),
        "factor_b": noise(keys[6], (JB, TJ, RANK), (TJ * TPD) ** -0.5, 0.5, ((1, 64),)),
        "factor_c": noise(keys[7], (KB, TK, RANK), TK ** -0.5, 0.75, ((1, 64),)),
    }


def device_partial(tiles, iblock, jslot, kslot, jlist, klist, factor_b, factor_c):
    def accumulate(which, partial_value):
        tile_block = tiles[which].astype(jnp.float32)
        mode_two = factor_b[jlist[jslot[which]]].astype(jnp.float32)
        mode_three = factor_c[klist[kslot[which]]].astype(jnp.float32)
        contracted = jnp.dot(tile_block.reshape(TI * TJ, TK), mode_three, precision=lax.Precision.HIGHEST)
        term = jnp.sum(contracted.reshape(TI, TJ, RANK) * mode_two[None], axis=1)
        target = iblock[which]
        current = lax.dynamic_index_in_dim(partial_value, target, 0, keepdims=False)
        return lax.dynamic_update_index_in_dim(partial_value, current + term, target, 0)

    partial_value = lax.fori_loop(0, TPD, accumulate, jnp.zeros((N_BLK, TI, RANK), jnp.float32))
    return lax.optimization_barrier(partial_value.astype(jnp.bfloat16)).astype(jnp.float32)


def reference(tensor_tiles, tile_iblock, tile_jslot, tile_kslot, block_jlist, block_klist, factor_b, factor_c):
    def column(column_index):
        tile_start = (column_index * TPD).astype(jnp.int32)
        list_start = (column_index * DIST).astype(jnp.int32)

        def row_partial(row_index):
            tiles = lax.dynamic_slice_in_dim(tensor_tiles[row_index], tile_start, TPD, 0)
            iblock = lax.dynamic_slice_in_dim(tile_iblock[row_index], tile_start, TPD, 0)
            jslot = lax.dynamic_slice_in_dim(tile_jslot[row_index], tile_start, TPD, 0)
            kslot = lax.dynamic_slice_in_dim(tile_kslot[row_index], tile_start, TPD, 0)
            jlist = lax.dynamic_slice_in_dim(block_jlist[row_index], list_start, DIST, 0)
            klist = lax.dynamic_slice_in_dim(block_klist[row_index], list_start, DIST, 0)
            return device_partial(tiles, iblock, jslot, kslot, jlist, klist, factor_b, factor_c)

        def add_row(total, row_index):
            return total + row_partial(row_index), None

        total, unused = lax.scan(add_row, jnp.zeros((N_BLK, TI, RANK), jnp.float32), jnp.arange(N_BLK, dtype=jnp.int32))
        return total

    blocks = lax.map(column, jnp.arange(N_TILES, dtype=jnp.int32))
    return jnp.transpose(blocks, (1, 0, 2, 3)).reshape(N_BLK * N_TILES * TI, RANK)
```

```python
import functools

import jax
import jax.numpy as jnp
from jax import lax
from jax.experimental import pallas as pl
from jax.experimental.pallas import tpu as pltpu
from jax.sharding import PartitionSpec as P

MESH = pl.DeviceIdType.MESH
F32 = jnp.float32
BF16 = jnp.bfloat16
LANES = 128
STAGE = 9


def one_hot(mask):
    return jnp.where(mask, 1.0, 0.0).astype(F32).astype(BF16)


def wait_bytes(ref, sem):
    pltpu.make_async_copy(ref, ref, sem).wait()


def kernel(
    groups, peers,
    tiles_hbm, iblock_hbm, jslot_hbm, kslot_hbm, jlist_hbm, klist_hbm, two_hbm, three_hbm,
    out_ref,
    iblock, jslot, kslot, jlist, klist, tiles, two, three,
    asked, mine, order, send_two, send_three, recv_two, recv_three, rows_two, rows_three,
    send_part, recv_part,
    local_sem, asked_sem, three_sem, two_sem, part_sem,
):
    count, inner, flat = tiles.shape
    rank = two.shape[1]
    across = peers
    chunks = rank // LANES
    slab = count * chunks
    me = lax.axis_index("tiles")
    row = lax.axis_index("blk")

    pairs = (
        (iblock_hbm, iblock), (jslot_hbm, jslot), (kslot_hbm, kslot), (jlist_hbm, jlist),
        (klist_hbm, klist), (three_hbm, three), (two_hbm, two), (tiles_hbm, tiles),
    )
    loads = [
        pltpu.make_async_copy(source, target, local_sem.at[index])
        for index, (source, target) in enumerate(pairs)
    ]
    for load in loads:
        load.start()

    barrier = pltpu.get_barrier_semaphore()

    def greet(step, carry):
        other = lax.rem(me + step, peers)
        pl.semaphore_signal(barrier, inc=1, device_id={"tiles": other}, device_id_type=MESH)
        return carry

    lax.fori_loop(1, peers, greet, 0)
    for step in range(1, groups):
        other = lax.rem(row + step, groups)
        pl.semaphore_signal(barrier, inc=1, device_id={"blk": other}, device_id_type=MESH)

    wide = peers * slab
    place = lax.broadcasted_iota(jnp.int32, (wide, wide), 0)
    column = lax.broadcasted_iota(jnp.int32, (wide, wide), 1)
    order[...] = one_hot(column == (place % peers) * slab + place // peers)

    for load in loads[:5]:
        load.wait()
    words = [
        jlist[0, jslot[0, which]] + klist[0, kslot[0, which]] * 65536 for which in range(count)
    ]
    lane = lax.broadcasted_iota(jnp.int32, (1, LANES), 1)
    message = jnp.where(lane < LANES // 2, words[0], words[1])
    mine[...] = message
    asked[pl.ds(me, 1)] = message.reshape(1, 1, LANES)

    pl.semaphore_wait(barrier, peers - 1 + groups - 1)
    if STAGE < 2:
        for load in loads[5:]:
            load.wait()
        out_ref[...] = jnp.zeros_like(out_ref)
        return

    def ask(step, carry):
        other = lax.rem(me + step, peers)
        pltpu.make_async_remote_copy(
            mine, asked.at[me], asked_sem.at[0], asked_sem.at[1],
            device_id={"tiles": other}, device_id_type=MESH,
        ).start()
        return carry

    lax.fori_loop(1, peers, ask, 0)
    for load in loads[5:7]:
        load.wait()
    wait_bytes(asked.at[pl.ds(0, peers - 1)], asked_sem.at[1])
    if STAGE < 3:
        wait_bytes(asked.at[pl.ds(0, peers - 1)], asked_sem.at[0])
        loads[7].wait()
        out_ref[...] = jnp.zeros_like(out_ref)
        return

    given = jnp.broadcast_to(asked[...], (peers, slab, LANES))
    turned = pltpu.roll(given.reshape(wide, LANES), LANES // 2, 1).reshape(peers, slab, LANES)
    sub = lax.broadcasted_iota(jnp.int32, (peers, slab, LANES), 1)
    lane = lax.broadcasted_iota(jnp.int32, (peers, slab, LANES), 2)
    word = jnp.where((sub < chunks) == (lane < LANES // 2), given, turned).reshape(wide, LANES)
    chunk = lax.broadcasted_iota(jnp.int32, (wide, LANES), 0) % chunks
    lane = lax.broadcasted_iota(jnp.int32, (wide, LANES), 1)

    def select(wanted, table):
        total = table.shape[0]
        key = wanted + chunk * total
        stacked = jnp.concatenate(
            [table[:, c * LANES : (c + 1) * LANES] for c in range(chunks)], axis=0
        )
        hot = jnp.concatenate(
            [one_hot(key == lane + start) for start in range(0, chunks * total, LANES)], axis=1
        )
        return jnp.dot(hot, stacked, preferred_element_type=F32).astype(BF16)

    def hand_out(send, recv, sem):
        def give(step, carry):
            other = lax.rem(me + step, peers)
            pltpu.make_async_remote_copy(
                send.at[other], recv.at[me], sem.at[0], sem.at[1],
                device_id={"tiles": other}, device_id_type=MESH,
            ).start()
            return carry

        lax.fori_loop(1, peers, give, 0)
        recv[pl.ds(me, 1)] = send[pl.ds(me, 1)]

    send_three[...] = select(lax.shift_right_logical(word, 16), three).reshape(peers, slab, LANES)
    if STAGE >= 4:
        hand_out(send_three, recv_three, three_sem)
    send_two[...] = select(lax.bitwise_and(word, 65535), two).reshape(peers, slab, LANES)
    if STAGE >= 4:
        hand_out(send_two, recv_two, two_sem)
    wait_bytes(asked.at[pl.ds(0, peers - 1)], asked_sem.at[0])
    loads[7].wait()
    if STAGE < 4:
        out_ref[...] = jnp.zeros_like(out_ref)
        return

    def arrange(recv, rows):
        sorted_rows = jnp.dot(
            order[...], recv[...].reshape(wide, LANES), preferred_element_type=F32
        )
        for which in range(count):
            for c in range(chunks):
                start = (which * chunks + c) * peers
                rows[which, :, c * LANES : (c + 1) * LANES] = sorted_rows[start : start + peers]

    some = pl.ds(0, peers - 1)
    wait_bytes(recv_three.at[some], three_sem.at[1])
    arrange(recv_three, rows_three)
    wait_bytes(recv_two.at[some], two_sem.at[1])
    arrange(recv_two, rows_two)
    wait_bytes(recv_three.at[some], three_sem.at[0])
    wait_bytes(recv_two.at[some], two_sem.at[0])
    if STAGE < 5:
        out_ref[...] = jnp.zeros_like(out_ref)
        return

    half = rank // 2
    together = 4
    depth = flat // across
    for part in range(2):
        columns = slice(part * half, (part + 1) * half)
        terms = []
        for which in range(count):
            mode_three = rows_three[which, :, columns]
            term = jnp.zeros((inner, half), F32)
            for first in range(0, across, together):
                product = jnp.concatenate(
                    [
                        (mode_three * rows_two[which, j : j + 1, columns]).astype(BF16)
                        for j in range(first, first + together)
                    ],
                    axis=0,
                )
                left = tiles[which, :, first * depth : (first + together) * depth]
                term = term + jnp.dot(left, product, preferred_element_type=F32)
            terms.append(term)
        for group in range(groups):
            total = jnp.zeros((inner, half), F32)
            for which in range(count):
                total = total + jnp.where(iblock[0, which] == group, terms[which], 0.0)
            send_part[part, group] = total.astype(BF16)
        if STAGE >= 6:
            for step in range(1, groups):
                other = lax.rem(row + step, groups)
                pltpu.make_async_remote_copy(
                    send_part.at[part, other], recv_part.at[part, row],
                    part_sem.at[0, part], part_sem.at[1, part],
                    device_id={"blk": other}, device_id_type=MESH,
                ).start()
            recv_part[part, pl.ds(row, 1)] = send_part[part, pl.ds(row, 1)]
    if STAGE < 6:
        out_ref[...] = jnp.concatenate([send_part[0, 0], send_part[1, 0]], axis=1).astype(F32)
        return

    for part in range(2):
        wait_bytes(recv_part.at[part, pl.ds(0, groups - 1)], part_sem.at[1, part])
        total = recv_part[part, 0].astype(F32)
        for group in range(1, groups):
            total = total + recv_part[part, group].astype(F32)
        out_ref[:, part * half : (part + 1) * half] = total
    for part in range(2):
        wait_bytes(send_part.at[part, pl.ds(0, groups - 1)], part_sem.at[0, part])


def per_device(
    tensor_tiles, tile_iblock, tile_jslot, tile_kslot, block_jlist, block_klist, factor_b, factor_c
):
    groups = lax.axis_size("blk")
    peers = lax.axis_size("tiles")
    tiles = tensor_tiles[0]
    two = factor_b.reshape(factor_b.shape[0], factor_b.shape[2])
    three = factor_c.reshape(factor_c.shape[0], factor_c.shape[2])
    count, inner, _ = tiles.shape
    rank = two.shape[1]
    slab = count * rank // LANES
    wide = peers * slab
    any_space = pl.BlockSpec(memory_space=pl.ANY)
    dma = pltpu.SemaphoreType.DMA
    rows = pltpu.VMEM((peers, slab, LANES), BF16)
    return pl.pallas_call(
        functools.partial(kernel, groups, peers),
        out_shape=jax.ShapeDtypeStruct((inner, rank), F32),
        in_specs=[any_space] * 8,
        out_specs=pl.BlockSpec(memory_space=pltpu.VMEM),
        scratch_shapes=[
            *[pltpu.SMEM((1, count), jnp.int32)] * 5,
            pltpu.VMEM(tiles.shape, BF16),
            pltpu.VMEM(two.shape, BF16),
            pltpu.VMEM(three.shape, BF16),
            pltpu.VMEM((peers, 1, LANES), jnp.int32),
            pltpu.VMEM((1, LANES), jnp.int32),
            pltpu.VMEM((wide, wide), BF16),
            rows, rows, rows, rows,
            pltpu.VMEM((count, peers, rank), F32),
            pltpu.VMEM((count, peers, rank), F32),
            pltpu.VMEM((2, groups, inner, rank // 2), BF16),
            pltpu.VMEM((2, groups, inner, rank // 2), BF16),
            dma((8,)), dma((2,)), dma((2,)), dma((2,)), dma((2, 2)),
        ],
        compiler_params=pltpu.CompilerParams(
            collective_id=0, has_side_effects=True, vmem_limit_bytes=40 * 1024 * 1024
        ),
    )(tiles, tile_iblock, tile_jslot, tile_kslot, block_jlist, block_klist, two, three)


def solution(mesh):
    placed = (
        P("blk", "tiles", None, None),
        P("blk", "tiles"),
        P("blk", "tiles"),
        P("blk", "tiles"),
        P("blk", "tiles"),
        P("blk", "tiles"),
        P(None, "tiles", None),
        P(None, "tiles", None),
    )
    return jax.shard_map(
        per_device, mesh=mesh, in_specs=placed, out_specs=P(("blk", "tiles"), None), check_vma=False
    )
```

```python
import functools

import jax
import jax.numpy as jnp
from jax import lax
from jax.experimental import pallas as pl
from jax.experimental.pallas import tpu as pltpu
from jax.sharding import PartitionSpec as P

MESH = pl.DeviceIdType.MESH
F32 = jnp.float32
BF16 = jnp.bfloat16
LANES = 128
STAGE = 9
EARLY = 4
SIDE = 4
REACH = 4


def one_hot(mask):
    return jnp.where(mask, 1.0, 0.0).astype(F32).astype(BF16)


def wait_bytes(ref, sem):
    pltpu.make_async_copy(ref, ref, sem).wait()


def spread(me, peers, visit):
    lanes = SIDE
    planes = peers // lanes

    def body(step, carry):
        turn, side = step // lanes, step % lanes
        away = (turn + 1) // 2
        far = planes // 2 + jnp.where(turn % 2 == 0, away, -away)
        plane = lax.rem(me // lanes + far, planes)
        other = plane * lanes + lax.rem(me + side, lanes)

        @pl.when(other != me)
        def _():
            visit(other)

        return carry

    lax.fori_loop(0, peers, body, 0)


def spread_early(me, peers, visit):
    early = EARLY * SIDE

    def body(other, carry):
        @pl.when(other != me)
        def _():
            visit(other)

        return carry

    lax.fori_loop(0, early, body, 0)

    def rest(other):
        @pl.when(other >= early)
        def _():
            visit(other)

    spread(me, peers, rest)


def kernel(
    groups, peers,
    tiles_hbm, iblock_hbm, jslot_hbm, kslot_hbm, jlist_hbm, klist_hbm, two_hbm, three_hbm,
    out_ref,
    iblock, jslot, kslot, jlist, klist, tiles, two, three,
    asked, order, send, recv, rows_two, rows_three,
    send_part, recv_part,
    local_sem, asked_sem, near_sem, rows_sem, part_sem,
):
    count, inner, flat = tiles.shape
    rank = two.shape[1]
    across = peers
    chunks = rank // LANES
    slab = count * chunks
    me = lax.axis_index("tiles")
    row = lax.axis_index("blk")

    pairs = (
        (iblock_hbm, iblock), (jslot_hbm, jslot), (kslot_hbm, kslot), (jlist_hbm, jlist),
        (klist_hbm, klist), (three_hbm, three), (two_hbm, two), (tiles_hbm, tiles),
    )
    loads = [
        pltpu.make_async_copy(source, target, local_sem.at[index])
        for index, (source, target) in enumerate(pairs)
    ]
    for load in loads:
        load.start()

    barrier = pltpu.get_barrier_semaphore()

    planes = peers // SIDE
    plane, lane_x = me // SIDE, lax.rem(me, SIDE)
    offsets = [sign * away for away in range(REACH, 0, -1) for sign in (1, -1)]

    def along(offset):
        return lax.rem(plane + (offset + planes), planes)

    def at_plane(offset):
        return {"tiles": along(offset) * SIDE + lane_x}

    def at_lane(step):
        return {"tiles": plane * SIDE + lax.rem(lane_x + step, SIDE)}

    def entry(offset):
        return asked.at[pl.ds(lane_x * planes + along(offset), 1)]

    for offset in offsets:
        pl.semaphore_signal(barrier, inc=1, device_id=at_plane(offset), device_id_type=MESH)
    for step in (2, 1, 3):
        pl.semaphore_signal(barrier, inc=1, device_id=at_lane(step), device_id_type=MESH)
    for step in range(1, groups):
        other = lax.rem(row + step, groups)
        pl.semaphore_signal(barrier, inc=1, device_id={"blk": other}, device_id_type=MESH)

    wide = peers * slab
    place = lax.broadcasted_iota(jnp.int32, (wide, wide), 0)
    column = lax.broadcasted_iota(jnp.int32, (wide, wide), 1)
    order[...] = one_hot(column == (place % peers) * slab + place // peers)

    for load in loads[:5]:
        load.wait()
    words = [
        jlist[0, jslot[0, which]] + klist[0, kslot[0, which]] * 65536 for which in range(count)
    ]
    lane = lax.broadcasted_iota(jnp.int32, (1, LANES), 1)
    message = jnp.where(lane < LANES // 2, words[0], words[1])
    asked[pl.ds(lane_x * planes + plane, 1)] = message.reshape(1, 1, LANES)

    pl.semaphore_wait(barrier, 2 * REACH + SIDE - 1 + groups - 1)
    if STAGE < 2:
        for load in loads[5:]:
            load.wait()
        out_ref[...] = jnp.zeros_like(out_ref)
        return

    def pass_on(what, sem, target):
        pltpu.make_async_remote_copy(
            what, what, asked_sem.at[0], sem, device_id=target, device_id_type=MESH
        ).start()

    for offset in offsets:
        pass_on(entry(0), near_sem.at[offset + REACH], at_plane(offset))
    for offset in offsets:
        wait_bytes(entry(-offset), near_sem.at[offset + REACH])
        if offset < 0:
            pass_on(entry(-offset), asked_sem.at[1], at_plane(-REACH))
        elif offset < REACH:
            pass_on(entry(-offset), asked_sem.at[1], at_plane(REACH))
    wait_bytes(asked.at[pl.ds(0, 2 * REACH - 1)], asked_sem.at[1])
    for step in (2, 1, 3):
        pass_on(asked.at[pl.ds(lane_x * planes, planes)], asked_sem.at[2], at_lane(step))
    for load in loads[5:7]:
        load.wait()
    wait_bytes(asked.at[pl.ds(0, peers - planes)], asked_sem.at[2])
    if STAGE < 3:
        wait_bytes(asked.at[pl.ds(0, peers - 1)], asked_sem.at[0])
        loads[7].wait()
        out_ref[...] = jnp.zeros_like(out_ref)
        return

    given = jnp.broadcast_to(asked[...], (peers, slab, LANES))
    turned = pltpu.roll(given.reshape(wide, LANES), LANES // 2, 1).reshape(peers, slab, LANES)
    sub = lax.broadcasted_iota(jnp.int32, (peers, slab, LANES), 1)
    lane = lax.broadcasted_iota(jnp.int32, (peers, slab, LANES), 2)
    word = jnp.where((sub < chunks) == (lane < LANES // 2), given, turned).reshape(wide, LANES)
    chunk = lax.broadcasted_iota(jnp.int32, (wide, LANES), 0) % chunks
    lane = lax.broadcasted_iota(jnp.int32, (wide, LANES), 1)

    def select(wanted, table):
        total = table.shape[0]
        key = wanted + chunk * total
        stacked = jnp.concatenate(
            [table[:, c * LANES : (c + 1) * LANES] for c in range(chunks)], axis=0
        )
        hot = jnp.concatenate(
            [one_hot(key == lane + start) for start in range(0, chunks * total, LANES)], axis=1
        )
        return jnp.dot(hot, stacked, preferred_element_type=F32).astype(BF16)

    send[:, 0] = select(lax.shift_right_logical(word, 16), three).reshape(peers, slab, LANES)
    send[:, 1] = select(lax.bitwise_and(word, 65535), two).reshape(peers, slab, LANES)

    def give(other):
        pltpu.make_async_remote_copy(
            send.at[lax.rem(other, SIDE) * planes + other // SIDE], recv.at[me], rows_sem.at[0], rows_sem.at[1],
            device_id={"tiles": other}, device_id_type=MESH,
        ).start()

    if STAGE >= 4:
        spread_early(me, peers, give)
        recv[pl.ds(me, 1)] = send[pl.ds(lane_x * planes + plane, 1)]
    wait_bytes(asked.at[pl.ds(0, peers - 1)], asked_sem.at[0])
    loads[7].wait()
    if STAGE < 4:
        out_ref[...] = jnp.zeros_like(out_ref)
        return

    def arrange(part, rows):
        sorted_rows = jnp.dot(
            order[...], recv[:, part].reshape(wide, LANES), preferred_element_type=F32
        )
        for which in range(count):
            for c in range(chunks):
                start = (which * chunks + c) * peers
                rows[which, :, c * LANES : (c + 1) * LANES] = sorted_rows[start : start + peers]

    some = pl.ds(0, peers - 1)
    wait_bytes(recv.at[some], rows_sem.at[1])
    arrange(0, rows_three)
    arrange(1, rows_two)
    wait_bytes(send.at[some], rows_sem.at[0])
    if STAGE < 5:
        out_ref[...] = jnp.zeros_like(out_ref)
        return

    half = rank // 2
    together = 4
    depth = flat // across
    for part in range(2):
        columns = slice(part * half, (part + 1) * half)
        terms = []
        for which in range(count):
            mode_three = rows_three[which, :, columns]
            term = jnp.zeros((inner, half), F32)
            for first in range(0, across, together):
                product = jnp.concatenate(
                    [
                        (mode_three * rows_two[which, j : j + 1, columns]).astype(BF16)
                        for j in range(first, first + together)
                    ],
                    axis=0,
                )
                left = tiles[which, :, first * depth : (first + together) * depth]
                term = term + jnp.dot(left, product, preferred_element_type=F32)
            terms.append(term)
        for group in range(groups):
            total = jnp.zeros((inner, half), F32)
            for which in range(count):
                total = total + jnp.where(iblock[0, which] == group, terms[which], 0.0)
            send_part[part, group] = total.astype(BF16)
        if STAGE >= 6:
            for step in range(1, groups):
                other = lax.rem(row + step, groups)
                pltpu.make_async_remote_copy(
                    send_part.at[part, other], recv_part.at[part, row],
                    part_sem.at[0, part], part_sem.at[1, part],
                    device_id={"blk": other}, device_id_type=MESH,
                ).start()
            recv_part[part, pl.ds(row, 1)] = send_part[part, pl.ds(row, 1)]
    if STAGE < 6:
        out_ref[...] = jnp.concatenate([send_part[0, 0], send_part[1, 0]], axis=1).astype(F32)
        return

    for part in range(2):
        wait_bytes(recv_part.at[part, pl.ds(0, groups - 1)], part_sem.at[1, part])
        total = recv_part[part, 0].astype(F32)
        for group in range(1, groups):
            total = total + recv_part[part, group].astype(F32)
        out_ref[:, part * half : (part + 1) * half] = total
    for part in range(2):
        wait_bytes(send_part.at[part, pl.ds(0, groups - 1)], part_sem.at[0, part])


def per_device(
    tensor_tiles, tile_iblock, tile_jslot, tile_kslot, block_jlist, block_klist, factor_b, factor_c
):
    groups = lax.axis_size("blk")
    peers = lax.axis_size("tiles")
    tiles = tensor_tiles[0]
    two = factor_b.reshape(factor_b.shape[0], factor_b.shape[2])
    three = factor_c.reshape(factor_c.shape[0], factor_c.shape[2])
    count, inner, _ = tiles.shape
    rank = two.shape[1]
    slab = count * rank // LANES
    wide = peers * slab
    any_space = pl.BlockSpec(memory_space=pl.ANY)
    dma = pltpu.SemaphoreType.DMA
    rows = pltpu.VMEM((peers, 2, slab, LANES), BF16)
    return pl.pallas_call(
        functools.partial(kernel, groups, peers),
        out_shape=jax.ShapeDtypeStruct((inner, rank), F32),
        in_specs=[any_space] * 8,
        out_specs=pl.BlockSpec(memory_space=pltpu.VMEM),
        scratch_shapes=[
            *[pltpu.SMEM((1, count), jnp.int32)] * 5,
            pltpu.VMEM(tiles.shape, BF16),
            pltpu.VMEM(two.shape, BF16),
            pltpu.VMEM(three.shape, BF16),
            pltpu.VMEM((peers, 1, LANES), jnp.int32),
            pltpu.VMEM((wide, wide), BF16),
            rows, rows,
            pltpu.VMEM((count, peers, rank), F32),
            pltpu.VMEM((count, peers, rank), F32),
            pltpu.VMEM((2, groups, inner, rank // 2), BF16),
            pltpu.VMEM((2, groups, inner, rank // 2), BF16),
            dma((8,)), dma((3,)), dma((2 * REACH + 1,)), dma((2,)), dma((2, 2)),
        ],
        compiler_params=pltpu.CompilerParams(
            collective_id=0, has_side_effects=True
        ),
    )(tiles, tile_iblock, tile_jslot, tile_kslot, block_jlist, block_klist, two, three)


def solution(mesh):
    placed = (
        P("blk", "tiles", None, None),
        P("blk", "tiles"),
        P("blk", "tiles"),
        P("blk", "tiles"),
        P("blk", "tiles"),
        P("blk", "tiles"),
        P(None, "tiles", None),
        P(None, "tiles", None),
    )
    return jax.shard_map(
        per_device, mesh=mesh, in_specs=placed, out_specs=P(("blk", "tiles"), None), check_vma=False
    )
```

```python
import functools

import jax
import jax.numpy as jnp
from jax import lax
from jax.experimental import pallas as pl
from jax.experimental.pallas import tpu as pltpu
from jax.sharding import PartitionSpec as P

MESH = pl.DeviceIdType.MESH
F32 = jnp.float32
BF16 = jnp.bfloat16
LANES = 128
SIDE = 4
CORES = 2
REACH = 4
EARLY = 4
FIRST = 12
STAGE = 9


def one_hot(mask):
    return jnp.where(mask, 1.0, 0.0).astype(F32).astype(BF16)


def wait_bytes(ref, sem):
    pltpu.make_async_copy(ref, ref, sem).wait()


def iota(shape, axis):
    return lax.broadcasted_iota(jnp.int32, shape, axis)


def kernel(
    groups, peers,
    tiles_hbm, iblock_hbm, jslot_hbm, kslot_hbm, jlist_hbm, klist_hbm, two_hbm, three_hbm,
    out_ref,
    iblock, jslot, kslot, jlist, klist, tiles, table,
    near, asked, order, send, recv, arranged, send_part, recv_part,
    local_sem, tile_sem, near_sem, asked_sem, rows_sem, part_sem, there_sem,
):
    count = iblock.shape[1]
    together = CORES * count
    inner, flat = tiles.shape[1:]
    half = table.shape[1]
    chunks = half // LANES
    slab = 2 * together
    height_two, height_three = two_hbm.shape[0], three_hbm.shape[0]
    planes = peers // SIDE
    me = lax.axis_index("tiles")
    row = lax.axis_index("blk")
    plane, lane_x = me // SIDE, lax.rem(me, SIDE)
    core = lax.rem(row, CORES)
    sibling = row + 1 - 2 * core

    def along(offset):
        return lax.rem(plane + (offset + planes), planes)

    def at_plane(offset):
        return {"tiles": along(offset) * SIDE + lane_x}

    beside = [{"blk": sibling}]
    for step in (2, 1, 3):
        other = plane * SIDE + lax.rem(lane_x + step, SIDE)
        beside += [{"tiles": other}, {"tiles": other, "blk": sibling}]
    owners = [lax.rem(row + step, groups) for step in range(1, groups)]
    close = [sign * away for away in range(REACH, 0, -1) for sign in (1, -1)]
    distant = [planes // 2] + [
        sign * away for away in range(planes // 2 - 1, REACH, -1) for sign in (1, -1)
    ]

    barrier = pltpu.get_barrier_semaphore()
    greeted = [at_plane(offset) for offset in close] + beside
    greeted += [
        {"blk": lax.rem(row + 2 * step + side, groups)}
        for step in range(1, groups // CORES) for side in (0, sibling - row)
    ]
    for target in greeted:
        pl.semaphore_signal(barrier, inc=1, device_id=target, device_id_type=MESH)

    pairs = [
        (iblock_hbm, iblock), (jslot_hbm, jslot), (kslot_hbm, kslot), (jlist_hbm, jlist),
        (klist_hbm, klist),
    ]
    columns = pl.ds(pl.multiple_of(core * half, half), half)
    pairs.append((two_hbm.at[:, columns], table.at[pl.ds(0, height_two)]))
    pairs.append((three_hbm.at[:, columns], table.at[pl.ds(height_two, height_three)]))
    mine = pl.ds(core * count, count)
    pairs.append((tiles_hbm, tiles.at[mine]))
    loads = [
        pltpu.make_async_copy(source, target, local_sem.at[index])
        for index, (source, target) in enumerate(pairs)
    ]
    for load in loads:
        load.start()
    for load in loads[:5]:
        load.wait()
    lane = iota((1, LANES), 1)
    message = jnp.zeros((1, LANES), jnp.int32)
    for which in range(count):
        spot = lane_x * together + core * count + which
        values = (jlist[0, jslot[0, which]], klist[0, kslot[0, which]], iblock[0, which])
        for kind, value in enumerate(values):
            message = jnp.where(lane == kind * SIDE * together + spot, value, message)
    position = pl.ds(lane_x * CORES + core, 1)
    near[position] = message.reshape(1, 1, LANES)

    pl.semaphore_wait(barrier, len(greeted))

    def copy(source, target, send_sem, recv_sem, device):
        pltpu.make_async_remote_copy(
            source, target, send_sem, recv_sem, device_id=device, device_id_type=MESH
        ).start()

    for offset in (REACH, -REACH):
        pl.semaphore_signal(there_sem, inc=1, device_id=at_plane(offset), device_id_type=MESH)
    for target in beside:
        copy(near.at[position], near.at[position], near_sem.at[0], near_sem.at[1], target)
    copy(tiles_hbm, tiles.at[mine], tile_sem.at[0], tile_sem.at[1], beside[0])

    wide = peers * slab
    order[...] = one_hot(
        iota((wide, wide), 1) == (iota((wide, wide), 0) % peers) * slab + iota((wide, wide), 0) // peers
    )

    wait_bytes(near.at[pl.ds(0, len(beside))], near_sem.at[1])
    asked[pl.ds(plane, 1)] = jnp.sum(near[...], axis=0, keepdims=True)

    spare = height_two + height_three
    table[spare:, :] = jnp.zeros((table.shape[0] - spare, half), BF16)

    def pass_on(origin, offset, away):
        entry = asked.at[pl.ds(origin, 1)]
        copy(entry, entry, asked_sem.at[planes], asked_sem.at[away % planes], at_plane(offset))

    for offset in close:
        pass_on(plane, offset, offset)

    @pl.when(plane >= EARLY)
    def _():
        pl.semaphore_wait(there_sem, 2)
        for offset in distant:
            pass_on(plane, offset, offset)

    def arrival(away):
        wait_bytes(asked.at[pl.ds(along(-away), 1)], asked_sem.at[away % planes])

    ahead = jnp.logical_and(plane >= REACH, plane < REACH + EARLY)
    behind = plane >= planes - REACH

    @pl.when(ahead)
    def _():
        arrival(REACH)
        for step in range(1, planes // 2 - REACH + 1):
            pass_on(along(-REACH), step, REACH + step)

    @pl.when(behind)
    def _():
        arrival(-REACH)
        for step in range(1, planes // 2 - REACH):
            pass_on(along(REACH), -step, -REACH - step)

    for load in loads[5:]:
        load.wait()
    rows = SIDE * slab

    def select(origins):
        total = rows * len(origins)
        given = jnp.concatenate(
            [jnp.broadcast_to(asked[origin], (rows, LANES)) for origin in origins], axis=0
        )
        place = iota((total, LANES), 0) % rows
        kind = place % slab // together
        spot = kind * SIDE * together + place // slab * together + place % together
        lane = iota((total, LANES), 1)
        wanted = jnp.sum(jnp.where(lane == spot, given, 0), axis=1, keepdims=True)
        key = wanted + kind * height_two
        hot = jnp.concatenate(
            [one_hot(key == lane + start) for start in range(0, table.shape[0], LANES)], axis=1
        )
        picked = jnp.dot(hot, table[...], preferred_element_type=F32).astype(BF16)
        for index, origin in enumerate(origins):
            for c in range(chunks):
                send[c, pl.ds(origin * SIDE, SIDE)] = picked[
                    index * rows : (index + 1) * rows, c * LANES : (c + 1) * LANES
                ].reshape(SIDE, slab, LANES)

    def give(c, origin, others=(2, 1, 3, 0)):
        for step in others:
            other = origin * SIDE + lax.rem(lane_x + step, SIDE)
            copy(
                send.at[c, other], recv.at[c, me], rows_sem.at[0, c], rows_sem.at[1, c],
                {"tiles": other},
            )

    def serve(origin, away, parts):
        known = jnp.logical_or(
            jnp.logical_and(ahead, away == REACH),
            jnp.logical_and(behind, away == planes - REACH),
        )

        @pl.when(jnp.logical_not(known))
        def _():
            wait_bytes(asked.at[pl.ds(origin, 1)], asked_sem.at[away])

        select([origin])
        for c in parts:
            give(c, origin)

    select([plane])
    for c in range(chunks):
        recv[c, pl.ds(me, 1)] = send[c, pl.ds(me, 1)]
        give(c, plane, (2, 1, 3))
    for origin in range(FIRST):
        away = lax.rem(plane + planes - origin, planes)

        @pl.when(plane != origin)
        def _():
            serve(origin, away, range(chunks))

    def others(offsets, visit):
        for offset in offsets:
            origin = along(-offset)

            @pl.when(origin >= FIRST)
            def _():
                visit(origin, offset % planes)

    others(reversed(close), lambda origin, away: serve(origin, away, range(chunks)))
    others(reversed(distant), lambda origin, away: serve(origin, away, (0,)))
    for c in range(1, chunks):
        others(reversed(distant), lambda origin, away: give(c, origin))

    wait_bytes(near.at[pl.ds(0, len(beside))], near_sem.at[0])
    wait_bytes(asked.at[pl.ds(0, 2 * REACH)], asked_sem.at[planes])

    @pl.when(plane >= EARLY)
    def _():
        wait_bytes(asked.at[pl.ds(0, planes - 1 - 2 * REACH)], asked_sem.at[planes])

    @pl.when(plane < EARLY)
    def _():
        pl.semaphore_wait(there_sem, 2)

    @pl.when(ahead)
    def _():
        wait_bytes(asked.at[pl.ds(0, planes // 2 - REACH)], asked_sem.at[planes])

    @pl.when(behind)
    def _():
        wait_bytes(asked.at[pl.ds(0, planes // 2 - REACH - 1)], asked_sem.at[planes])

    wait_bytes(tiles.at[pl.ds(0, count)], tile_sem.at[1])
    wait_bytes(tiles.at[pl.ds(0, count)], tile_sem.at[0])

    some = pl.ds(0, peers - 1)
    step = 4
    depth = flat // peers
    summary = asked[plane]
    homes = []
    for which in range(together):
        spot = 2 * SIDE * together + lane_x * together + which
        homes.append(jnp.sum(jnp.where(lane == spot, summary, 0), axis=1, keepdims=True))
    for c in range(chunks):
        wait_bytes(recv.at[c, some], rows_sem.at[1, c])
        arranged[...] = jnp.dot(
            order[...], recv[c].reshape(wide, LANES), preferred_element_type=F32
        )
        if STAGE < 5:
            continue
        terms = []
        for which in range(together):
            top = which * peers
            mode_three = arranged[(together + which) * peers : (together + which + 1) * peers, :]
            term = jnp.zeros((inner, LANES), F32)
            for first in range(0, peers, step):
                product = jnp.concatenate(
                    [
                        (mode_three * arranged[top + j : top + j + 1, :]).astype(BF16)
                        for j in range(first, first + step)
                    ],
                    axis=0,
                )
                left = tiles[which, :, first * depth : (first + step) * depth]
                term = term + jnp.dot(left, product, preferred_element_type=F32)
            terms.append(term)
        for group in range(groups):
            total = jnp.zeros((inner, LANES), F32)
            for which in range(together):
                total = total + jnp.where(homes[which] == group, terms[which], 0.0)
            send_part[c, group] = total.astype(BF16)
        if STAGE < 6:
            continue
        for other in owners:
            copy(
                send_part.at[c, other], recv_part.at[c, row], part_sem.at[0, c],
                part_sem.at[1, c], {"blk": other},
            )
        recv_part[c, pl.ds(row, 1)] = send_part[c, pl.ds(row, 1)]
    for c in range(chunks):
        wait_bytes(send.at[c, some], rows_sem.at[0, c])
    if STAGE < 6:
        out_ref[...] = jnp.zeros_like(out_ref)
        return
    for c in range(chunks):
        wait_bytes(recv_part.at[c, pl.ds(0, groups - 1)], part_sem.at[1, c])
        for side in range(CORES):
            total = recv_part[c, side].astype(F32)
            for group in range(side + CORES, groups, CORES):
                total = total + recv_part[c, group].astype(F32)
            start = side * half + c * LANES
            out_ref[:, start : start + LANES] = total
    for c in range(chunks):
        wait_bytes(send_part.at[c, pl.ds(0, groups - 1)], part_sem.at[0, c])


def per_device(
    tensor_tiles, tile_iblock, tile_jslot, tile_kslot, block_jlist, block_klist, factor_b, factor_c
):
    groups = lax.axis_size("blk")
    peers = lax.axis_size("tiles")
    tiles = tensor_tiles[0]
    two = factor_b.reshape(factor_b.shape[0], factor_b.shape[2])
    three = factor_c.reshape(factor_c.shape[0], factor_c.shape[2])
    count, inner, flat = tiles.shape
    together = CORES * count
    rank = two.shape[1]
    half = rank // CORES
    chunks = half // LANES
    slab = 2 * together
    wide = peers * slab
    planes = peers // SIDE
    height = -(-(two.shape[0] + three.shape[0]) // LANES) * LANES
    dma = pltpu.SemaphoreType.DMA
    exchanged = pltpu.VMEM((chunks, peers, slab, LANES), BF16)
    part = pltpu.VMEM((chunks, groups, inner, LANES), BF16)
    return pl.pallas_call(
        functools.partial(kernel, groups, peers),
        out_shape=jax.ShapeDtypeStruct((inner, rank), F32),
        in_specs=[pl.BlockSpec(memory_space=pl.ANY)] * 8,
        out_specs=pl.BlockSpec(memory_space=pltpu.VMEM),
        scratch_shapes=[
            *[pltpu.SMEM((1, count), jnp.int32)] * 5,
            pltpu.VMEM((together, inner, flat), BF16),
            pltpu.VMEM((height, half), BF16),
            pltpu.VMEM((SIDE * CORES, 1, LANES), jnp.int32),
            pltpu.VMEM((planes, 1, LANES), jnp.int32),
            pltpu.VMEM((wide, wide), BF16),
            exchanged, exchanged, pltpu.VMEM((wide, LANES), F32), part, part,
            dma((8,)), dma((2,)), dma((2,)), dma((planes + 1,)), dma((2, chunks)), dma((2, chunks)),
            pltpu.SemaphoreType.REGULAR,
        ],
        compiler_params=pltpu.CompilerParams(collective_id=0, has_side_effects=True),
    )(tiles, tile_iblock, tile_jslot, tile_kslot, block_jlist, block_klist, two, three)


def solution(mesh):
    placed = (
        P("blk", "tiles", None, None),
        P("blk", "tiles"),
        P("blk", "tiles"),
        P("blk", "tiles"),
        P("blk", "tiles"),
        P("blk", "tiles"),
        P(None, "tiles", None),
        P(None, "tiles", None),
    )
    return jax.shard_map(
        per_device, mesh=mesh, in_specs=placed, out_specs=P(("blk", "tiles"), None), check_vma=False
    )
```

```python
import functools

import jax
import jax.numpy as jnp
from jax import lax
from jax.experimental import pallas as pl
from jax.experimental.pallas import tpu as pltpu
from jax.sharding import PartitionSpec as P

MESH = pl.DeviceIdType.MESH
F32 = jnp.float32
BF16 = jnp.bfloat16
LANES = 128
SIDE = 4
CORES = 2
REACH = 4
HOP = 2
FIRST = 8
AHEAD = 6
STAGE = 9


def one_hot(mask):
    return jnp.where(mask, 1.0, 0.0).astype(F32).astype(BF16)


def wait_bytes(ref, sem):
    pltpu.make_async_copy(ref, ref, sem).wait()


def iota(shape, axis):
    return lax.broadcasted_iota(jnp.int32, shape, axis)


def kernel(
    groups, peers,
    tiles_hbm, iblock_hbm, jslot_hbm, kslot_hbm, jlist_hbm, klist_hbm, two_hbm, three_hbm,
    out_ref,
    iblock, jslot, kslot, jlist, klist, tiles, table,
    near, asked, order, send, recv, arranged, send_part, recv_part,
    local_sem, tile_sem, near_sem, asked_sem, rows_sem, part_sem, there_sem, chain_sem,
):
    count = iblock.shape[1]
    together = CORES * count
    inner, flat = tiles.shape[1:]
    half = table.shape[1]
    chunks = half // LANES
    slab = 2 * together
    height_two, height_three = two_hbm.shape[0], three_hbm.shape[0]
    planes = peers // SIDE
    me = lax.axis_index("tiles")
    row = lax.axis_index("blk")
    plane, lane_x = me // SIDE, lax.rem(me, SIDE)
    core = lax.rem(row, CORES)
    sibling = row + 1 - 2 * core

    def along(offset):
        return lax.rem(plane + (offset + planes), planes)

    def at_plane(offset):
        return {"tiles": along(offset) * SIDE + lane_x}

    beside = [{"blk": sibling}]
    for step in (2, 1, 3):
        other = plane * SIDE + lax.rem(lane_x + step, SIDE)
        beside += [{"tiles": other}, {"tiles": other, "blk": sibling}]
    owners = [lax.rem(row + step, groups) for step in range(1, groups)]
    close = [sign * away for away in range(REACH, 0, -1) for sign in (1, -1)]
    distant = [planes // 2] + [
        sign * away for away in range(planes // 2 - 1, REACH, -1) for sign in (1, -1)
    ]

    barrier = pltpu.get_barrier_semaphore()
    split = planes // 2
    late = plane >= split

    def below(offset):
        return jnp.logical_and(along(offset) < split, along(offset) < plane)

    def above(offset):
        return jnp.logical_and(plane < split, along(offset) > plane)

    def both_late(offset):
        return jnp.logical_and(late, along(offset) >= split)

    def signal(sem, target):
        pl.semaphore_signal(sem, inc=1, device_id=target, device_id_type=MESH)

    for offset in close:
        told = jnp.logical_and(above(offset), along(offset) < split)
        if abs(offset) <= HOP:
            told = jnp.logical_or(told, both_late(offset))
        pl.when(told)(lambda: signal(barrier, at_plane(offset)))
    greeted = beside + [
        {"blk": lax.rem(row + 2 * step + side, groups)}
        for step in range(1, groups // CORES) for side in (0, sibling - row)
    ]
    for target in greeted:
        signal(barrier, target)

    pairs = [
        (iblock_hbm, iblock), (jslot_hbm, jslot), (kslot_hbm, kslot), (jlist_hbm, jlist),
        (klist_hbm, klist),
    ]
    columns = pl.ds(pl.multiple_of(core * half, half), half)
    pairs.append((two_hbm.at[:, columns], table.at[pl.ds(0, height_two)]))
    pairs.append((three_hbm.at[:, columns], table.at[pl.ds(height_two, height_three)]))
    mine = pl.ds(core * count, count)
    pairs.append((tiles_hbm, tiles.at[mine]))
    loads = [
        pltpu.make_async_copy(source, target, local_sem.at[index])
        for index, (source, target) in enumerate(pairs)
    ]
    for load in loads:
        load.start()
    for load in loads[:5]:
        load.wait()
    lane = iota((1, LANES), 1)
    message = jnp.zeros((1, LANES), jnp.int32)
    for which in range(count):
        spot = lane_x * together + core * count + which
        values = (jlist[0, jslot[0, which]], klist[0, kslot[0, which]], iblock[0, which])
        for kind, value in enumerate(values):
            message = jnp.where(lane == kind * SIDE * together + spot, value, message)
    position = pl.ds(lane_x * CORES + core, 1)
    near[position] = message.reshape(1, 1, LANES)

    expected = len(greeted)
    for offset in close:
        due = below(offset)
        if abs(offset) <= HOP:
            due = jnp.logical_or(due, both_late(offset))
        expected = expected + jnp.where(due, 1, 0)
    pl.semaphore_wait(barrier, expected)
    for offset in close:
        told = jnp.logical_and(above(offset), along(offset) >= split)
        pl.when(told)(lambda: signal(barrier, at_plane(offset)))

    def copy(source, target, send_sem, recv_sem, device):
        pltpu.make_async_remote_copy(
            source, target, send_sem, recv_sem, device_id=device, device_id_type=MESH
        ).start()

    def chain(step):
        for offset in (HOP, -HOP):
            target = {"tiles": along(offset) * SIDE + lane_x}
            pl.when(both_late(offset))(lambda: signal(chain_sem.at[step], target))

    def chain_wait(step):
        links = sum(jnp.where(both_late(offset), 1, 0) for offset in (HOP, -HOP))
        pl.when(late)(lambda: pl.semaphore_wait(chain_sem.at[step], links))

    chain(0)
    for offset in close:
        pl.when(below(offset))(lambda: signal(there_sem.at[-offset % planes], at_plane(offset)))
    for target in beside:
        copy(near.at[position], near.at[position], near_sem.at[0], near_sem.at[1], target)
    copy(tiles_hbm, tiles.at[mine], tile_sem.at[0], tile_sem.at[1], beside[0])

    wide = peers * slab
    order[...] = one_hot(
        iota((wide, wide), 1) == (iota((wide, wide), 0) % peers) * slab + iota((wide, wide), 0) // peers
    )

    spare = height_two + height_three
    table[spare:, :] = jnp.zeros((table.shape[0] - spare, half), BF16)
    chain_wait(0)
    chain(1)
    wait_bytes(near.at[pl.ds(0, len(beside))], near_sem.at[1])
    asked[pl.ds(plane, 1)] = jnp.sum(near[...], axis=0, keepdims=True)

    def pass_on(origin, offset, away):
        entry = asked.at[pl.ds(origin, 1)]
        copy(entry, entry, asked_sem.at[planes], asked_sem.at[away % planes], at_plane(offset))

    def arrival(away):
        wait_bytes(asked.at[pl.ds(along(-away), 1)], asked_sem.at[away % planes])

    for offset in close:
        pl.when(jnp.logical_or(late, below(offset)))(lambda: pass_on(plane, offset, offset))
    for offset in sorted(close, key=lambda offset: offset % planes if offset > 0 else planes - offset):
        @pl.when(above(offset))
        def _():
            pl.semaphore_wait(there_sem.at[offset % planes], 1)
            pass_on(plane, offset, offset)

    nearer = [offset for offset in distant if abs(offset) <= 3 * HOP]
    farther = [offset for offset in distant if abs(offset) > 3 * HOP]
    for step, offsets in ((1, nearer), (2, farther)):
        chain_wait(step)
        if step == 1:
            chain(2)

        @pl.when(late)
        def _():
            for offset in offsets:
                pass_on(plane, offset, offset)

    ahead = jnp.logical_and(plane >= REACH, plane < planes - REACH)
    behind = jnp.logical_not(ahead)

    @pl.when(ahead)
    def _():
        arrival(REACH)

        @pl.when(along(-REACH) < split)
        def _():
            for step in range(1, AHEAD + 1):
                pass_on(along(-REACH), step, REACH + step)

    @pl.when(behind)
    def _():
        arrival(-REACH)

        @pl.when(along(REACH) < split)
        def _():
            for step in range(1, 2 * (split - REACH) - AHEAD):
                pass_on(along(REACH), -step, -REACH - step)

    for load in loads[5:]:
        load.wait()
    rows = SIDE * slab

    def select(origins):
        total = rows * len(origins)
        given = jnp.concatenate(
            [jnp.broadcast_to(asked[origin], (rows, LANES)) for origin in origins], axis=0
        )
        place = iota((total, LANES), 0) % rows
        kind = place % slab // together
        spot = kind * SIDE * together + place // slab * together + place % together
        lane = iota((total, LANES), 1)
        wanted = jnp.sum(jnp.where(lane == spot, given, 0), axis=1, keepdims=True)
        key = wanted + kind * height_two
        hot = jnp.concatenate(
            [one_hot(key == lane + start) for start in range(0, table.shape[0], LANES)], axis=1
        )
        picked = jnp.dot(hot, table[...], preferred_element_type=F32).astype(BF16)
        for index, origin in enumerate(origins):
            for c in range(chunks):
                send[c, pl.ds(origin * SIDE, SIDE)] = picked[
                    index * rows : (index + 1) * rows, c * LANES : (c + 1) * LANES
                ].reshape(SIDE, slab, LANES)

    def give(c, origin, others=(2, 1, 3, 0)):
        for step in others:
            other = origin * SIDE + lax.rem(lane_x + step, SIDE)
            copy(
                send.at[c, other], recv.at[c, me], rows_sem.at[0, c], rows_sem.at[1, c],
                {"tiles": other},
            )

    def serve(origin, away, parts):
        known = jnp.logical_or(
            jnp.logical_and(ahead, away == REACH),
            jnp.logical_and(behind, away == planes - REACH),
        )

        @pl.when(jnp.logical_not(known))
        def _():
            wait_bytes(asked.at[pl.ds(origin, 1)], asked_sem.at[away])

        select([origin])
        for c in parts:
            give(c, origin)

    select([plane])
    for c in range(chunks):
        recv[c, pl.ds(me, 1)] = send[c, pl.ds(me, 1)]
        give(c, plane, (2, 1, 3))
    for origin in range(FIRST):
        away = lax.rem(plane + planes - origin, planes)

        @pl.when(plane != origin)
        def _():
            serve(origin, away, range(chunks))

    def others(offsets, visit):
        for offset in offsets:
            origin = along(-offset)

            @pl.when(origin >= FIRST)
            def _():
                visit(origin, offset % planes)

    near_first = list(reversed(close))
    far_first = distant
    others(near_first, lambda origin, away: serve(origin, away, (0,)))
    others(reversed(distant), lambda origin, away: serve(origin, away, (0,)))
    others(far_first, lambda origin, away: give(1, origin))
    others(close, lambda origin, away: give(1, origin))

    wait_bytes(near.at[pl.ds(0, len(beside))], near_sem.at[0])
    wait_bytes(asked.at[pl.ds(0, 2 * REACH)], asked_sem.at[planes])

    @pl.when(late)
    def _():
        wait_bytes(asked.at[pl.ds(0, planes - 1 - 2 * REACH)], asked_sem.at[planes])

    @pl.when(jnp.logical_and(ahead, along(-REACH) < split))
    def _():
        wait_bytes(asked.at[pl.ds(0, AHEAD)], asked_sem.at[planes])

    @pl.when(jnp.logical_and(behind, along(REACH) < split))
    def _():
        wait_bytes(asked.at[pl.ds(0, 2 * (split - REACH) - AHEAD - 1)], asked_sem.at[planes])

    wait_bytes(tiles.at[pl.ds(0, count)], tile_sem.at[1])
    wait_bytes(tiles.at[pl.ds(0, count)], tile_sem.at[0])

    some = pl.ds(0, peers - 1)
    step = 4
    depth = flat // peers
    summary = asked[plane]
    homes = []
    for which in range(together):
        spot = 2 * SIDE * together + lane_x * together + which
        homes.append(jnp.sum(jnp.where(lane == spot, summary, 0), axis=1, keepdims=True))
    for c in range(chunks):
        wait_bytes(recv.at[c, some], rows_sem.at[1, c])
        arranged[...] = jnp.dot(
            order[...], recv[c].reshape(wide, LANES), preferred_element_type=F32
        )
        if STAGE < 5:
            continue
        terms = []
        for which in range(together):
            top = which * peers
            mode_three = arranged[(together + which) * peers : (together + which + 1) * peers, :]
            term = jnp.zeros((inner, LANES), F32)
            for first in range(0, peers, step):
                product = jnp.concatenate(
                    [
                        (mode_three * arranged[top + j : top + j + 1, :]).astype(BF16)
                        for j in range(first, first + step)
                    ],
                    axis=0,
                )
                left = tiles[which, :, first * depth : (first + step) * depth]
                term = term + jnp.dot(left, product, preferred_element_type=F32)
            terms.append(term)
        for group in range(groups):
            total = jnp.zeros((inner, LANES), F32)
            for which in range(together):
                total = total + jnp.where(homes[which] == group, terms[which], 0.0)
            send_part[c, group] = total.astype(BF16)
        if STAGE < 6:
            continue
        for other in owners:
            copy(
                send_part.at[c, other], recv_part.at[c, row], part_sem.at[0, c],
                part_sem.at[1, c], {"blk": other},
            )
        recv_part[c, pl.ds(row, 1)] = send_part[c, pl.ds(row, 1)]
    for c in range(chunks):
        wait_bytes(send.at[c, some], rows_sem.at[0, c])
    if STAGE < 6:
        out_ref[...] = jnp.zeros_like(out_ref)
        return
    for c in range(chunks):
        wait_bytes(recv_part.at[c, pl.ds(0, groups - 1)], part_sem.at[1, c])
        for side in range(CORES):
            total = recv_part[c, side].astype(F32)
            for group in range(side + CORES, groups, CORES):
                total = total + recv_part[c, group].astype(F32)
            start = side * half + c * LANES
            out_ref[:, start : start + LANES] = total
    for c in range(chunks):
        wait_bytes(send_part.at[c, pl.ds(0, groups - 1)], part_sem.at[0, c])


def per_device(
    tensor_tiles, tile_iblock, tile_jslot, tile_kslot, block_jlist, block_klist, factor_b, factor_c
):
    groups = lax.axis_size("blk")
    peers = lax.axis_size("tiles")
    tiles = tensor_tiles[0]
    two = factor_b.reshape(factor_b.shape[0], factor_b.shape[2])
    three = factor_c.reshape(factor_c.shape[0], factor_c.shape[2])
    count, inner, flat = tiles.shape
    together = CORES * count
    rank = two.shape[1]
    half = rank // CORES
    chunks = half // LANES
    slab = 2 * together
    wide = peers * slab
    planes = peers // SIDE
    height = -(-(two.shape[0] + three.shape[0]) // LANES) * LANES
    dma = pltpu.SemaphoreType.DMA
    exchanged = pltpu.VMEM((chunks, peers, slab, LANES), BF16)
    part = pltpu.VMEM((chunks, groups, inner, LANES), BF16)
    return pl.pallas_call(
        functools.partial(kernel, groups, peers),
        out_shape=pltpu.VMEM((inner, rank), F32),
        in_specs=[pl.BlockSpec(memory_space=pl.ANY)] * 8,
        out_specs=pl.BlockSpec(memory_space=pltpu.VMEM),
        scratch_shapes=[
            *[pltpu.SMEM((1, count), jnp.int32)] * 5,
            pltpu.VMEM((together, inner, flat), BF16),
            pltpu.VMEM((height, half), BF16),
            pltpu.VMEM((SIDE * CORES, 1, LANES), jnp.int32),
            pltpu.VMEM((planes, 1, LANES), jnp.int32),
            pltpu.VMEM((wide, wide), BF16),
            exchanged, exchanged, pltpu.VMEM((wide, LANES), F32), part, part,
            dma((8,)), dma((2,)), dma((2,)), dma((planes + 1,)), dma((2, chunks)), dma((2, chunks)),
            pltpu.SemaphoreType.REGULAR((planes,)), pltpu.SemaphoreType.REGULAR((3,)),
        ],
        compiler_params=pltpu.CompilerParams(collective_id=0, has_side_effects=True),
    )(tiles, tile_iblock, tile_jslot, tile_kslot, block_jlist, block_klist, two, three)


def solution(mesh):
    placed = (
        P("blk", "tiles", None, None),
        P("blk", "tiles"),
        P("blk", "tiles"),
        P("blk", "tiles"),
        P("blk", "tiles"),
        P("blk", "tiles"),
        P(None, "tiles", None),
        P(None, "tiles", None),
    )
    return jax.shard_map(
        per_device, mesh=mesh, in_specs=placed, out_specs=P(("blk", "tiles"), None), check_vma=False
    )
```

```python
import functools

import jax
import jax.numpy as jnp
from jax import lax
from jax.experimental import pallas as pl
from jax.experimental.pallas import tpu as pltpu
from jax.sharding import PartitionSpec as P

MESH = pl.DeviceIdType.MESH
F32 = jnp.float32
BF16 = jnp.bfloat16
LANES = 128
SIDE = 4
CORES = 2
REACH = 4
HOP = 2
FIRST = 8
AHEAD = 6
STEP = 4


def one_hot(mask):
    return jnp.where(mask, 1.0, 0.0).astype(F32).astype(BF16)


def wait_bytes(ref, sem):
    pltpu.make_async_copy(ref, ref, sem).wait()


def iota(shape, axis):
    return lax.broadcasted_iota(jnp.int32, shape, axis)


def kernel(
    groups, peers,
    tiles_hbm, iblock_hbm, jslot_hbm, kslot_hbm, jlist_hbm, klist_hbm, two_hbm, three_hbm,
    out_ref,
    iblock, jslot, kslot, jlist, klist, tiles, table,
    near, asked, order, send, recv, arranged, send_part, recv_part,
    local_sem, tile_sem, near_sem, asked_sem, rows_sem, part_sem, there_sem, chain_sem,
):
    count = iblock.shape[1]
    together = CORES * count
    inner, flat = tiles.shape[1:]
    half = table.shape[1]
    chunks = half // LANES
    slab = 2 * together
    height_two, height_three = two_hbm.shape[0], three_hbm.shape[0]
    planes = peers // SIDE
    me = lax.axis_index("tiles")
    row = lax.axis_index("blk")
    plane, lane_x = me // SIDE, lax.rem(me, SIDE)
    core = lax.rem(row, CORES)
    sibling = row + 1 - 2 * core

    def along(offset):
        return lax.rem(plane + (offset + planes), planes)

    def at_plane(offset):
        return {"tiles": along(offset) * SIDE + lane_x}

    beside = [{"blk": sibling}]
    for step in (2, 1, 3):
        other = plane * SIDE + lax.rem(lane_x + step, SIDE)
        beside += [{"tiles": other}, {"tiles": other, "blk": sibling}]
    owners = [lax.rem(row + step, groups) for step in range(1, groups)]
    close = [sign * away for away in range(REACH, 0, -1) for sign in (1, -1)]
    distant = [planes // 2] + [
        sign * away for away in range(planes // 2 - 1, REACH, -1) for sign in (1, -1)
    ]

    barrier = pltpu.get_barrier_semaphore()
    split = planes // 2
    late = plane >= split

    def below(offset):
        return jnp.logical_and(along(offset) < split, along(offset) < plane)

    def above(offset):
        return jnp.logical_and(plane < split, along(offset) > plane)

    def both_late(offset):
        return jnp.logical_and(late, along(offset) >= split)

    def signal(sem, target):
        pl.semaphore_signal(sem, inc=1, device_id=target, device_id_type=MESH)

    for offset in close:
        told = jnp.logical_and(above(offset), along(offset) < split)
        if abs(offset) <= HOP:
            told = jnp.logical_or(told, both_late(offset))
        pl.when(told)(lambda: signal(barrier, at_plane(offset)))
    greeted = beside + [
        {"blk": lax.rem(row + 2 * step + side, groups)}
        for step in range(1, groups // CORES) for side in (0, sibling - row)
    ]
    for target in greeted:
        signal(barrier, target)

    pairs = [
        (iblock_hbm, iblock), (jslot_hbm, jslot), (kslot_hbm, kslot), (jlist_hbm, jlist),
        (klist_hbm, klist),
    ]
    columns = pl.ds(pl.multiple_of(core * half, half), half)
    pairs.append((two_hbm.at[:, columns], table.at[pl.ds(0, height_two)]))
    pairs.append((three_hbm.at[:, columns], table.at[pl.ds(height_two, height_three)]))
    mine = pl.ds(core * count, count)
    pairs.append((tiles_hbm, tiles.at[mine]))
    loads = [
        pltpu.make_async_copy(source, target, local_sem.at[index])
        for index, (source, target) in enumerate(pairs)
    ]
    for load in loads:
        load.start()
    for load in loads[:5]:
        load.wait()
    lane = iota((1, LANES), 1)
    message = jnp.zeros((1, LANES), jnp.int32)
    for which in range(count):
        spot = lane_x * together + core * count + which
        values = (jlist[0, jslot[0, which]], klist[0, kslot[0, which]], iblock[0, which])
        for kind, value in enumerate(values):
            message = jnp.where(lane == kind * SIDE * together + spot, value, message)
    position = pl.ds(lane_x * CORES + core, 1)
    near[position] = message.reshape(1, 1, LANES)

    expected = len(greeted)
    for offset in close:
        due = below(offset)
        if abs(offset) <= HOP:
            due = jnp.logical_or(due, both_late(offset))
        expected = expected + jnp.where(due, 1, 0)
    pl.semaphore_wait(barrier, expected)
    for offset in close:
        told = jnp.logical_and(above(offset), along(offset) >= split)
        pl.when(told)(lambda: signal(barrier, at_plane(offset)))

    def copy(source, target, send_sem, recv_sem, device):
        pltpu.make_async_remote_copy(
            source, target, send_sem, recv_sem, device_id=device, device_id_type=MESH
        ).start()

    def chain(step):
        for offset in (HOP, -HOP):
            target = {"tiles": along(offset) * SIDE + lane_x}
            pl.when(both_late(offset))(lambda: signal(chain_sem.at[step], target))

    def chain_wait(step):
        links = sum(jnp.where(both_late(offset), 1, 0) for offset in (HOP, -HOP))
        pl.when(late)(lambda: pl.semaphore_wait(chain_sem.at[step], links))

    chain(0)
    for offset in close:
        pl.when(below(offset))(lambda: signal(there_sem.at[-offset % planes], at_plane(offset)))
    for target in beside:
        copy(near.at[position], near.at[position], near_sem.at[0], near_sem.at[1], target)
    copy(tiles_hbm, tiles.at[mine], tile_sem.at[0], tile_sem.at[1], beside[0])

    wide = peers * slab
    order[...] = one_hot(
        iota((wide, wide), 1) == (iota((wide, wide), 0) % peers) * slab + iota((wide, wide), 0) // peers
    )

    spare = height_two + height_three
    table[spare:, :] = jnp.zeros((table.shape[0] - spare, half), BF16)
    chain_wait(0)
    chain(1)
    wait_bytes(near.at[pl.ds(0, len(beside))], near_sem.at[1])
    asked[pl.ds(plane, 1)] = jnp.sum(near[...], axis=0, keepdims=True)

    def pass_on(origin, offset, away):
        entry = asked.at[pl.ds(origin, 1)]
        copy(entry, entry, asked_sem.at[planes], asked_sem.at[away % planes], at_plane(offset))

    def arrival(away):
        wait_bytes(asked.at[pl.ds(along(-away), 1)], asked_sem.at[away % planes])

    for offset in close:
        pl.when(jnp.logical_or(late, below(offset)))(lambda: pass_on(plane, offset, offset))
    for offset in sorted(close, key=lambda offset: offset % planes if offset > 0 else planes - offset):
        @pl.when(above(offset))
        def _():
            pl.semaphore_wait(there_sem.at[offset % planes], 1)
            pass_on(plane, offset, offset)

    def to_early(offset):
        return along(offset) < split

    def soon(offset):
        sure = jnp.logical_and(to_early(offset), plane < planes - HOP)
        if offset == split - 1:
            sure = jnp.logical_and(sure, plane != split + 1)
        return sure

    def ask_distant(when):
        for offset in distant:
            pl.when(jnp.logical_and(late, when(offset)))(lambda: pass_on(plane, offset, offset))

    ask_distant(soon)
    chain_wait(1)
    chain(2)
    ask_distant(
        lambda offset: jnp.logical_and(
            jnp.logical_not(soon(offset)),
            to_early(offset) if abs(offset) > 3 * HOP else True,
        )
    )
    chain_wait(2)
    ask_distant(
        lambda offset: jnp.logical_not(to_early(offset)) if abs(offset) > 3 * HOP else False
    )

    ahead = jnp.logical_and(plane >= REACH, plane < planes - REACH)
    behind = jnp.logical_not(ahead)

    @pl.when(ahead)
    def _():
        arrival(REACH)

        @pl.when(along(-REACH) < split)
        def _():
            for step in range(1, AHEAD + 1):
                pass_on(along(-REACH), step, REACH + step)

    @pl.when(behind)
    def _():
        arrival(-REACH)

        @pl.when(along(REACH) < split)
        def _():
            for step in range(1, 2 * (split - REACH) - AHEAD):
                pass_on(along(REACH), -step, -REACH - step)

    for load in loads[5:]:
        load.wait()
    rows = SIDE * slab

    def select(origins):
        total = rows * len(origins)
        given = jnp.concatenate(
            [jnp.broadcast_to(asked[origin], (rows, LANES)) for origin in origins], axis=0
        )
        place = iota((total, LANES), 0) % rows
        kind = place % slab // together
        spot = kind * SIDE * together + place // slab * together + place % together
        lane = iota((total, LANES), 1)
        wanted = jnp.sum(jnp.where(lane == spot, given, 0), axis=1, keepdims=True)
        key = wanted + kind * height_two
        hot = jnp.concatenate(
            [one_hot(key == lane + start) for start in range(0, table.shape[0], LANES)], axis=1
        )
        picked = jnp.dot(hot, table[...], preferred_element_type=F32).astype(BF16)
        for index, origin in enumerate(origins):
            for c in range(chunks):
                send[c, pl.ds(origin * SIDE, SIDE)] = picked[
                    index * rows : (index + 1) * rows, c * LANES : (c + 1) * LANES
                ].reshape(SIDE, slab, LANES)

    def give(c, origin, others=(2, 1, 3, 0)):
        for step in others:
            other = origin * SIDE + lax.rem(lane_x + step, SIDE)
            copy(
                send.at[c, other], recv.at[c, me], rows_sem.at[0, c], rows_sem.at[1, c],
                {"tiles": other},
            )

    def serve(origin, away, parts):
        known = jnp.logical_or(
            jnp.logical_and(ahead, away == REACH),
            jnp.logical_and(behind, away == planes - REACH),
        )

        @pl.when(jnp.logical_not(known))
        def _():
            wait_bytes(asked.at[pl.ds(origin, 1)], asked_sem.at[away])

        select([origin])
        for c in parts:
            give(c, origin)

    select([plane])
    for c in range(chunks):
        recv[c, pl.ds(me, 1)] = send[c, pl.ds(me, 1)]
        give(c, plane, (2, 1, 3))
    for origin in range(FIRST):
        away = lax.rem(plane + planes - origin, planes)

        @pl.when(plane != origin)
        def _():
            serve(origin, away, range(chunks))

    def others(offsets, visit):
        for offset in offsets:
            origin = along(-offset)

            @pl.when(origin >= FIRST)
            def _():
                visit(origin, offset % planes)

    near_first = list(reversed(close))
    far_first = distant
    others(near_first, lambda origin, away: serve(origin, away, (0,)))
    others(reversed(distant), lambda origin, away: serve(origin, away, (0,)))
    others(far_first, lambda origin, away: give(1, origin))
    others(close, lambda origin, away: give(1, origin))

    wait_bytes(near.at[pl.ds(0, len(beside))], near_sem.at[0])
    wait_bytes(asked.at[pl.ds(0, 2 * REACH)], asked_sem.at[planes])

    @pl.when(late)
    def _():
        wait_bytes(asked.at[pl.ds(0, planes - 1 - 2 * REACH)], asked_sem.at[planes])

    @pl.when(jnp.logical_and(ahead, along(-REACH) < split))
    def _():
        wait_bytes(asked.at[pl.ds(0, AHEAD)], asked_sem.at[planes])

    @pl.when(jnp.logical_and(behind, along(REACH) < split))
    def _():
        wait_bytes(asked.at[pl.ds(0, 2 * (split - REACH) - AHEAD - 1)], asked_sem.at[planes])

    wait_bytes(tiles.at[pl.ds(0, count)], tile_sem.at[1])
    wait_bytes(tiles.at[pl.ds(0, count)], tile_sem.at[0])

    some = pl.ds(0, peers - 1)
    step = STEP
    depth = flat // peers
    summary = asked[plane]
    homes = []
    for which in range(together):
        spot = 2 * SIDE * together + lane_x * together + which
        homes.append(jnp.sum(jnp.where(lane == spot, summary, 0), axis=1, keepdims=True))
    for c in range(chunks):
        wait_bytes(recv.at[c, some], rows_sem.at[1, c])
        arranged[...] = jnp.dot(
            order[...], recv[c].reshape(wide, LANES), preferred_element_type=F32
        ).astype(BF16)
        terms = []
        for pair in range(0, together, 2):
            both = (pair, pair + 1)
            term = jnp.zeros((2 * inner, 2 * LANES), F32)
            for first in range(0, peers, step):
                product = jnp.concatenate(
                    [
                        jnp.concatenate(
                            [
                                arranged[(together + which) * peers : (together + which + 1) * peers, :]
                                * arranged[which * peers + j : which * peers + j + 1, :]
                                for which in both
                            ],
                            axis=1,
                        )
                        for j in range(first, first + step)
                    ],
                    axis=0,
                )
                left = jnp.concatenate(
                    [tiles[which, :, first * depth : (first + step) * depth] for which in both],
                    axis=0,
                )
                term = term + jnp.dot(left, product, preferred_element_type=F32)
            terms += [term[:inner, :LANES], term[inner:, LANES:]]
        for group in range(groups):
            total = jnp.zeros((inner, LANES), F32)
            for which in range(together):
                total = total + jnp.where(homes[which] == group, terms[which], 0.0)
            send_part[c, group] = total.astype(BF16)
        for other in owners:
            copy(
                send_part.at[c, other], recv_part.at[c, row], part_sem.at[0, c],
                part_sem.at[1, c], {"blk": other},
            )
        recv_part[c, pl.ds(row, 1)] = send_part[c, pl.ds(row, 1)]
    for c in range(chunks):
        wait_bytes(recv_part.at[c, pl.ds(0, groups - 1)], part_sem.at[1, c])
        for side in range(CORES):
            total = recv_part[c, side].astype(F32)
            for group in range(side + CORES, groups, CORES):
                total = total + recv_part[c, group].astype(F32)
            start = side * half + c * LANES
            out_ref[:, start : start + LANES] = total
    for c in range(chunks):
        wait_bytes(send.at[c, some], rows_sem.at[0, c])
        wait_bytes(send_part.at[c, pl.ds(0, groups - 1)], part_sem.at[0, c])


def per_device(
    tensor_tiles, tile_iblock, tile_jslot, tile_kslot, block_jlist, block_klist, factor_b, factor_c
):
    groups = lax.axis_size("blk")
    peers = lax.axis_size("tiles")
    tiles = tensor_tiles[0]
    two = factor_b.reshape(factor_b.shape[0], factor_b.shape[2])
    three = factor_c.reshape(factor_c.shape[0], factor_c.shape[2])
    count, inner, flat = tiles.shape
    together = CORES * count
    rank = two.shape[1]
    half = rank // CORES
    chunks = half // LANES
    slab = 2 * together
    wide = peers * slab
    planes = peers // SIDE
    height = -(-(two.shape[0] + three.shape[0]) // LANES) * LANES
    dma = pltpu.SemaphoreType.DMA
    exchanged = pltpu.VMEM((chunks, peers, slab, LANES), BF16)
    part = pltpu.VMEM((chunks, groups, inner, LANES), BF16)
    return pl.pallas_call(
        functools.partial(kernel, groups, peers),
        out_shape=pltpu.VMEM((inner, rank), F32),
        in_specs=[pl.BlockSpec(memory_space=pl.ANY)] * 8,
        out_specs=pl.BlockSpec(memory_space=pltpu.VMEM),
        scratch_shapes=[
            *[pltpu.SMEM((1, count), jnp.int32)] * 5,
            pltpu.VMEM((together, inner, flat), BF16),
            pltpu.VMEM((height, half), BF16),
            pltpu.VMEM((SIDE * CORES, 1, LANES), jnp.int32),
            pltpu.VMEM((planes, 1, LANES), jnp.int32),
            pltpu.VMEM((wide, wide), BF16),
            exchanged, exchanged, pltpu.VMEM((wide, LANES), BF16), part, part,
            dma((8,)), dma((2,)), dma((2,)), dma((planes + 1,)), dma((2, chunks)), dma((2, chunks)),
            pltpu.SemaphoreType.REGULAR((planes,)), pltpu.SemaphoreType.REGULAR((3,)),
        ],
        compiler_params=pltpu.CompilerParams(collective_id=0, has_side_effects=True),
    )(tiles, tile_iblock, tile_jslot, tile_kslot, block_jlist, block_klist, two, three)


def solution(mesh):
    placed = (
        P("blk", "tiles", None, None),
        P("blk", "tiles"),
        P("blk", "tiles"),
        P("blk", "tiles"),
        P("blk", "tiles"),
        P("blk", "tiles"),
        P(None, "tiles", None),
        P(None, "tiles", None),
    )
    return jax.shard_map(
        per_device, mesh=mesh, in_specs=placed, out_specs=P(("blk", "tiles"), None), check_vma=False
    )
```

```python
import functools

import jax
import jax.numpy as jnp
from jax import lax
from jax.experimental import pallas as pl
from jax.experimental.pallas import tpu as pltpu
from jax.sharding import PartitionSpec as P

MESH = pl.DeviceIdType.MESH
F32 = jnp.float32
BF16 = jnp.bfloat16
LANES = 128
SIDE = 4
CORES = 2
REACH = 4
HOP = 2
FIRST = 8
AHEAD = 6
STEP = 4


def one_hot(mask):
    return jnp.where(mask, 1.0, 0.0).astype(F32).astype(BF16)


def wait_bytes(ref, sem):
    pltpu.make_async_copy(ref, ref, sem).wait()


def iota(shape, axis):
    return lax.broadcasted_iota(jnp.int32, shape, axis)


def kernel(
    groups, peers,
    tiles_hbm, iblock_hbm, jslot_hbm, kslot_hbm, jlist_hbm, klist_hbm, two_hbm, three_hbm,
    out_ref,
    iblock, jslot, kslot, jlist, klist, tiles, table,
    near, asked, order, send, recv, arranged, send_part, recv_part,
    local_sem, tile_sem, near_sem, asked_sem, rows_sem, part_sem, there_sem, chain_sem,
):
    count = iblock.shape[1]
    together = CORES * count
    inner, flat = tiles.shape[1:]
    half = table.shape[1]
    chunks = half // LANES
    slab = 2 * together
    height_two, height_three = two_hbm.shape[0], three_hbm.shape[0]
    planes = peers // SIDE
    me = lax.axis_index("tiles")
    row = lax.axis_index("blk")
    plane, lane_x = me // SIDE, lax.rem(me, SIDE)
    core = lax.rem(row, CORES)
    sibling = row + 1 - 2 * core

    def along(offset):
        return lax.rem(plane + (offset + planes), planes)

    def at_plane(offset):
        return {"tiles": along(offset) * SIDE + lane_x}

    beside = [{"blk": sibling}]
    for step in (2, 1, 3):
        other = plane * SIDE + lax.rem(lane_x + step, SIDE)
        beside += [{"tiles": other}, {"tiles": other, "blk": sibling}]
    owners = [lax.rem(row + step, groups) for step in (4, 5, 3, 2, 6, 7, 1)]
    close = [sign * away for away in range(REACH, 0, -1) for sign in (1, -1)]
    distant = [planes // 2] + [
        sign * away for away in range(planes // 2 - 1, REACH, -1) for sign in (1, -1)
    ]

    barrier = pltpu.get_barrier_semaphore()
    split = planes // 2
    late = plane >= split

    def below(offset):
        return jnp.logical_and(along(offset) < split, along(offset) < plane)

    def above(offset):
        return jnp.logical_and(plane < split, along(offset) > plane)

    def both_late(offset):
        return jnp.logical_and(late, along(offset) >= split)

    def signal(sem, target):
        pl.semaphore_signal(sem, inc=1, device_id=target, device_id_type=MESH)

    for offset in close:
        told = jnp.logical_and(above(offset), along(offset) < split)
        if abs(offset) <= HOP:
            told = jnp.logical_or(told, both_late(offset))
        pl.when(told)(lambda: signal(barrier, at_plane(offset)))
    greeted = beside + [
        {"blk": lax.rem(row + 2 * step + side, groups)}
        for step in range(1, groups // CORES) for side in (0, sibling - row)
    ]
    for target in greeted:
        signal(barrier, target)

    pairs = [
        (iblock_hbm, iblock), (jslot_hbm, jslot), (kslot_hbm, kslot), (jlist_hbm, jlist),
        (klist_hbm, klist),
    ]
    columns = pl.ds(pl.multiple_of(core * half, half), half)
    pairs.append((two_hbm.at[:, columns], table.at[pl.ds(0, height_two)]))
    pairs.append((three_hbm.at[:, columns], table.at[pl.ds(height_two, height_three)]))
    mine = pl.ds(core * count, count)
    pairs.append((tiles_hbm, tiles.at[mine]))
    loads = [
        pltpu.make_async_copy(source, target, local_sem.at[index])
        for index, (source, target) in enumerate(pairs)
    ]
    for load in loads:
        load.start()
    for load in loads[:5]:
        load.wait()
    lane = iota((1, LANES), 1)
    message = jnp.zeros((1, LANES), jnp.int32)
    for which in range(count):
        spot = lane_x * together + core * count + which
        values = (jlist[0, jslot[0, which]], klist[0, kslot[0, which]], iblock[0, which])
        for kind, value in enumerate(values):
            message = jnp.where(lane == kind * SIDE * together + spot, value, message)
    position = pl.ds(lane_x * CORES + core, 1)
    near[position] = message.reshape(1, 1, LANES)

    wide = peers * slab
    order[...] = one_hot(
        iota((wide, wide), 1) == (iota((wide, wide), 0) % peers) * slab + iota((wide, wide), 0) // peers
    )

    expected = len(greeted)
    for offset in close:
        due = below(offset)
        if abs(offset) <= HOP:
            due = jnp.logical_or(due, both_late(offset))
        expected = expected + jnp.where(due, 1, 0)
    pl.semaphore_wait(barrier, expected)
    for offset in close:
        told = jnp.logical_and(above(offset), along(offset) >= split)
        pl.when(told)(lambda: signal(barrier, at_plane(offset)))

    def copy(source, target, send_sem, recv_sem, device):
        pltpu.make_async_remote_copy(
            source, target, send_sem, recv_sem, device_id=device, device_id_type=MESH
        ).start()

    def chain(step):
        for offset in (HOP, -HOP):
            target = {"tiles": along(offset) * SIDE + lane_x}
            pl.when(both_late(offset))(lambda: signal(chain_sem.at[step], target))

    def chain_wait(step):
        links = sum(jnp.where(both_late(offset), 1, 0) for offset in (HOP, -HOP))
        pl.when(late)(lambda: pl.semaphore_wait(chain_sem.at[step], links))

    chain(0)
    for offset in close:
        pl.when(below(offset))(lambda: signal(there_sem.at[-offset % planes], at_plane(offset)))
    for target in beside:
        copy(near.at[position], near.at[position], near_sem.at[0], near_sem.at[1], target)
    copy(tiles_hbm, tiles.at[mine], tile_sem.at[0], tile_sem.at[1], beside[0])

    spare = height_two + height_three
    table[spare:, :] = jnp.zeros((table.shape[0] - spare, half), BF16)
    chain_wait(0)
    chain(1)
    wait_bytes(near.at[pl.ds(0, len(beside))], near_sem.at[1])
    asked[pl.ds(plane, 1)] = jnp.sum(near[...], axis=0, keepdims=True)

    def pass_on(origin, offset, away):
        entry = asked.at[pl.ds(origin, 1)]
        copy(entry, entry, asked_sem.at[planes], asked_sem.at[away % planes], at_plane(offset))

    def arrival(away):
        wait_bytes(asked.at[pl.ds(along(-away), 1)], asked_sem.at[away % planes])

    for offset in close:
        pl.when(jnp.logical_or(late, below(offset)))(lambda: pass_on(plane, offset, offset))
    for offset in sorted(close, key=lambda offset: offset % planes if offset > 0 else planes - offset):
        @pl.when(above(offset))
        def _():
            pl.semaphore_wait(there_sem.at[offset % planes], 1)
            pass_on(plane, offset, offset)

    def to_early(offset):
        return along(offset) < split

    def soon(offset):
        sure = jnp.logical_and(to_early(offset), plane < planes - HOP)
        if offset == split - 1:
            sure = jnp.logical_and(sure, plane != split + 1)
        return sure

    def ask_distant(when):
        for offset in distant:
            pl.when(jnp.logical_and(late, when(offset)))(lambda: pass_on(plane, offset, offset))

    ask_distant(soon)
    chain_wait(1)
    chain(2)
    ask_distant(
        lambda offset: jnp.logical_and(
            jnp.logical_not(soon(offset)),
            to_early(offset) if abs(offset) > 3 * HOP else True,
        )
    )
    chain_wait(2)
    ask_distant(
        lambda offset: jnp.logical_not(to_early(offset)) if abs(offset) > 3 * HOP else False
    )

    ahead = jnp.logical_and(plane >= REACH, plane < planes - REACH)
    behind = jnp.logical_not(ahead)

    @pl.when(ahead)
    def _():
        arrival(REACH)

        @pl.when(along(-REACH) < split)
        def _():
            for step in range(1, AHEAD + 1):
                pass_on(along(-REACH), step, REACH + step)

    @pl.when(behind)
    def _():
        arrival(-REACH)

        @pl.when(along(REACH) < split)
        def _():
            for step in range(1, 2 * (split - REACH) - AHEAD):
                pass_on(along(REACH), -step, -REACH - step)

    for load in loads[5:]:
        load.wait()
    rows = SIDE * slab

    def select(origins):
        total = rows * len(origins)
        given = jnp.concatenate(
            [jnp.broadcast_to(asked[origin], (rows, LANES)) for origin in origins], axis=0
        )
        place = iota((total, LANES), 0) % rows
        kind = place % slab // together
        spot = kind * SIDE * together + place // slab * together + place % together
        lane = iota((total, LANES), 1)
        wanted = jnp.sum(jnp.where(lane == spot, given, 0), axis=1, keepdims=True)
        key = wanted + kind * height_two
        hot = jnp.concatenate(
            [one_hot(key == lane + start) for start in range(0, table.shape[0], LANES)], axis=1
        )
        picked = jnp.dot(hot, table[...], preferred_element_type=F32).astype(BF16)
        for index, origin in enumerate(origins):
            for c in range(chunks):
                send[c, pl.ds(origin * SIDE, SIDE)] = picked[
                    index * rows : (index + 1) * rows, c * LANES : (c + 1) * LANES
                ].reshape(SIDE, slab, LANES)

    def give(c, origin, others=(2, 1, 3, 0)):
        for step in others:
            other = origin * SIDE + lax.rem(lane_x + step, SIDE)
            copy(
                send.at[c, other], recv.at[c, me], rows_sem.at[0, c], rows_sem.at[1, c],
                {"tiles": other},
            )

    def serve(origin, away, parts):
        known = jnp.logical_or(
            jnp.logical_and(ahead, away == REACH),
            jnp.logical_and(behind, away == planes - REACH),
        )

        @pl.when(jnp.logical_not(known))
        def _():
            wait_bytes(asked.at[pl.ds(origin, 1)], asked_sem.at[away])

        select([origin])
        for c in parts:
            give(c, origin)

    select([plane])
    for c in range(chunks):
        recv[c, pl.ds(me, 1)] = send[c, pl.ds(me, 1)]
        give(c, plane, (2, 1, 3))
    for origin in range(FIRST):
        away = lax.rem(plane + planes - origin, planes)

        @pl.when(plane != origin)
        def _():
            serve(origin, away, range(chunks))

    def others(offsets, visit):
        for offset in offsets:
            origin = along(-offset)

            @pl.when(origin >= FIRST)
            def _():
                visit(origin, offset % planes)

    near_first = list(reversed(close))
    far_first = distant
    others(near_first, lambda origin, away: serve(origin, away, (0,)))
    others(reversed(distant), lambda origin, away: serve(origin, away, (0,)))
    others(far_first, lambda origin, away: give(1, origin))
    others(close, lambda origin, away: give(1, origin))

    wait_bytes(near.at[pl.ds(0, len(beside))], near_sem.at[0])
    wait_bytes(asked.at[pl.ds(0, 2 * REACH)], asked_sem.at[planes])

    @pl.when(late)
    def _():
        wait_bytes(asked.at[pl.ds(0, planes - 1 - 2 * REACH)], asked_sem.at[planes])

    @pl.when(jnp.logical_and(ahead, along(-REACH) < split))
    def _():
        wait_bytes(asked.at[pl.ds(0, AHEAD)], asked_sem.at[planes])

    @pl.when(jnp.logical_and(behind, along(REACH) < split))
    def _():
        wait_bytes(asked.at[pl.ds(0, 2 * (split - REACH) - AHEAD - 1)], asked_sem.at[planes])

    wait_bytes(tiles.at[pl.ds(0, count)], tile_sem.at[1])
    wait_bytes(tiles.at[pl.ds(0, count)], tile_sem.at[0])

    some = pl.ds(0, peers - 1)
    step = STEP
    depth = flat // peers
    summary = asked[plane]
    homes = []
    for which in range(together):
        spot = 2 * SIDE * together + lane_x * together + which
        homes.append(jnp.sum(jnp.where(lane == spot, summary, 0), axis=1, keepdims=True))
    for c in range(chunks):
        wait_bytes(recv.at[c, some], rows_sem.at[1, c])
        arranged[...] = jnp.dot(
            order[...], recv[c].reshape(wide, LANES), preferred_element_type=F32
        ).astype(BF16)
        terms = []
        for pair in range(0, together, 2):
            both = (pair, pair + 1)
            term = jnp.zeros((2 * inner, 2 * LANES), F32)
            for first in range(0, peers, step):
                product = jnp.concatenate(
                    [
                        jnp.concatenate(
                            [
                                arranged[(together + which) * peers : (together + which + 1) * peers, :]
                                * arranged[which * peers + j : which * peers + j + 1, :]
                                for which in both
                            ],
                            axis=1,
                        )
                        for j in range(first, first + step)
                    ],
                    axis=0,
                )
                left = jnp.concatenate(
                    [tiles[which, :, first * depth : (first + step) * depth] for which in both],
                    axis=0,
                )
                term = term + jnp.dot(left, product, preferred_element_type=F32)
            terms += [term[:inner, :LANES], term[inner:, LANES:]]
        def partial(group):
            total = jnp.zeros((inner, LANES), F32)
            for which in range(together):
                total = total + jnp.where(homes[which] == group, terms[which], 0.0)
            return total.astype(BF16)

        for other in owners:
            send_part[c, pl.ds(other, 1)] = partial(other).reshape(1, inner, LANES)
            copy(
                send_part.at[c, other], recv_part.at[c, row], part_sem.at[0, c],
                part_sem.at[1, c], {"blk": other},
            )
        recv_part[c, pl.ds(row, 1)] = partial(row).reshape(1, inner, LANES)
    for c in range(chunks):
        wait_bytes(recv_part.at[c, pl.ds(0, groups - 1)], part_sem.at[1, c])
        for side in range(CORES):
            total = recv_part[c, side].astype(F32)
            for group in range(side + CORES, groups, CORES):
                total = total + recv_part[c, group].astype(F32)
            start = side * half + c * LANES
            out_ref[:, start : start + LANES] = total
    for c in range(chunks):
        wait_bytes(send.at[c, some], rows_sem.at[0, c])
        wait_bytes(send_part.at[c, pl.ds(0, groups - 1)], part_sem.at[0, c])


def per_device(
    tensor_tiles, tile_iblock, tile_jslot, tile_kslot, block_jlist, block_klist, factor_b, factor_c
):
    groups = lax.axis_size("blk")
    peers = lax.axis_size("tiles")
    tiles = tensor_tiles[0]
    two = factor_b.reshape(factor_b.shape[0], factor_b.shape[2])
    three = factor_c.reshape(factor_c.shape[0], factor_c.shape[2])
    count, inner, flat = tiles.shape
    together = CORES * count
    rank = two.shape[1]
    half = rank // CORES
    chunks = half // LANES
    slab = 2 * together
    wide = peers * slab
    planes = peers // SIDE
    height = -(-(two.shape[0] + three.shape[0]) // LANES) * LANES
    dma = pltpu.SemaphoreType.DMA
    exchanged = pltpu.VMEM((chunks, peers, slab, LANES), BF16)
    part = pltpu.VMEM((chunks, groups, inner, LANES), BF16)
    return pl.pallas_call(
        functools.partial(kernel, groups, peers),
        out_shape=pltpu.VMEM((inner, rank), F32),
        in_specs=[pl.BlockSpec(memory_space=pl.ANY)] * 8,
        out_specs=pl.BlockSpec(memory_space=pltpu.VMEM),
        scratch_shapes=[
            *[pltpu.SMEM((1, count), jnp.int32)] * 5,
            pltpu.VMEM((together, inner, flat), BF16),
            pltpu.VMEM((height, half), BF16),
            pltpu.VMEM((SIDE * CORES, 1, LANES), jnp.int32),
            pltpu.VMEM((planes, 1, LANES), jnp.int32),
            pltpu.VMEM((wide, wide), BF16),
            exchanged, exchanged, pltpu.VMEM((wide, LANES), BF16), part, part,
            dma((8,)), dma((2,)), dma((2,)), dma((planes + 1,)), dma((2, chunks)), dma((2, chunks)),
            pltpu.SemaphoreType.REGULAR((planes,)), pltpu.SemaphoreType.REGULAR((3,)),
        ],
        compiler_params=pltpu.CompilerParams(collective_id=0, has_side_effects=True),
    )(tiles, tile_iblock, tile_jslot, tile_kslot, block_jlist, block_klist, two, three)


def solution(mesh):
    placed = (
        P("blk", "tiles", None, None),
        P("blk", "tiles"),
        P("blk", "tiles"),
        P("blk", "tiles"),
        P("blk", "tiles"),
        P("blk", "tiles"),
        P(None, "tiles", None),
        P(None, "tiles", None),
    )
    return jax.shard_map(
        per_device, mesh=mesh, in_specs=placed, out_specs=P(("blk", "tiles"), None), check_vma=False
    )
```

```python
import functools

import jax
import jax.numpy as jnp
from jax import lax
from jax.experimental import pallas as pl
from jax.experimental.pallas import tpu as pltpu
from jax.sharding import PartitionSpec as P

MESH = pl.DeviceIdType.MESH
F32 = jnp.float32
BF16 = jnp.bfloat16
LANES = 128
SIDE = 4
CORES = 2
REACH = 4
HOP = 2
FIRST = 12
AHEAD = 6
STEP = 4


def one_hot(mask):
    return jnp.where(mask, 1.0, 0.0).astype(F32).astype(BF16)


def wait_bytes(ref, sem):
    pltpu.make_async_copy(ref, ref, sem).wait()


def iota(shape, axis):
    return lax.broadcasted_iota(jnp.int32, shape, axis)


def kernel(
    groups, peers,
    tiles_hbm, iblock_hbm, jslot_hbm, kslot_hbm, jlist_hbm, klist_hbm, two_hbm, three_hbm,
    out_ref,
    iblock, jslot, kslot, jlist, klist, tiles, table,
    near, asked, order, send, recv, arranged, send_part, recv_part,
    local_sem, tile_sem, near_sem, asked_sem, rows_sem, part_sem, there_sem, chain_sem,
):
    count = iblock.shape[1]
    together = CORES * count
    inner, flat = tiles.shape[1:]
    half = table.shape[1]
    chunks = half // LANES
    slab = 2 * together
    height_two, height_three = two_hbm.shape[0], three_hbm.shape[0]
    planes = peers // SIDE
    me = lax.axis_index("tiles")
    row = lax.axis_index("blk")
    plane, lane_x = me // SIDE, lax.rem(me, SIDE)
    core = lax.rem(row, CORES)
    sibling = row + 1 - 2 * core

    def along(offset):
        return lax.rem(plane + (offset + planes), planes)

    def at_plane(offset):
        return {"tiles": along(offset) * SIDE + lane_x}

    beside = [{"blk": sibling}]
    for step in (2, 1, 3):
        other = plane * SIDE + lax.rem(lane_x + step, SIDE)
        beside += [{"tiles": other}, {"tiles": other, "blk": sibling}]
    owners = [lax.rem(row + step, groups) for step in (4, 5, 3, 2, 6, 7, 1)]
    close = [sign * away for away in range(REACH, 0, -1) for sign in (1, -1)]
    distant = [planes // 2] + [
        sign * away for away in range(planes // 2 - 1, REACH, -1) for sign in (1, -1)
    ]

    barrier = pltpu.get_barrier_semaphore()
    split = planes // 2
    late = plane >= split

    def below(offset):
        return jnp.logical_and(along(offset) < split, along(offset) < plane)

    def above(offset):
        return jnp.logical_and(plane < split, along(offset) > plane)

    def both_late(offset):
        return jnp.logical_and(late, along(offset) >= split)

    def signal(sem, target):
        pl.semaphore_signal(sem, inc=1, device_id=target, device_id_type=MESH)

    for offset in close:
        told = jnp.logical_and(above(offset), along(offset) < split)
        if abs(offset) <= HOP:
            told = jnp.logical_or(told, both_late(offset))
        pl.when(told)(lambda: signal(barrier, at_plane(offset)))
    greeted = beside + [
        {"blk": lax.rem(row + 2 * step + side, groups)}
        for step in range(1, groups // CORES) for side in (0, sibling - row)
    ]
    for target in greeted:
        signal(barrier, target)

    pairs = [
        (iblock_hbm, iblock), (jslot_hbm, jslot), (kslot_hbm, kslot), (jlist_hbm, jlist),
        (klist_hbm, klist),
    ]
    columns = pl.ds(pl.multiple_of(core * half, half), half)
    pairs.append((two_hbm.at[:, columns], table.at[pl.ds(0, height_two)]))
    pairs.append((three_hbm.at[:, columns], table.at[pl.ds(height_two, height_three)]))
    mine = pl.ds(core * count, count)
    pairs.append((tiles_hbm, tiles.at[mine]))
    loads = [
        pltpu.make_async_copy(source, target, local_sem.at[index])
        for index, (source, target) in enumerate(pairs)
    ]
    for load in loads:
        load.start()
    for load in loads[:5]:
        load.wait()
    lane = iota((1, LANES), 1)
    message = jnp.zeros((1, LANES), jnp.int32)
    for which in range(count):
        spot = lane_x * together + core * count + which
        values = (jlist[0, jslot[0, which]], klist[0, kslot[0, which]], iblock[0, which])
        for kind, value in enumerate(values):
            message = jnp.where(lane == kind * SIDE * together + spot, value, message)
    position = pl.ds(lane_x * CORES + core, 1)
    near[position] = message.reshape(1, 1, LANES)

    wide = peers * slab
    order[...] = one_hot(
        iota((wide, wide), 1) == (iota((wide, wide), 0) % peers) * slab + iota((wide, wide), 0) // peers
    )

    expected = len(greeted)
    for offset in close:
        due = below(offset)
        if abs(offset) <= HOP:
            due = jnp.logical_or(due, both_late(offset))
        expected = expected + jnp.where(due, 1, 0)
    pl.semaphore_wait(barrier, expected)
    for offset in close:
        told = jnp.logical_and(above(offset), along(offset) >= split)
        pl.when(told)(lambda: signal(barrier, at_plane(offset)))

    def copy(source, target, send_sem, recv_sem, device):
        pltpu.make_async_remote_copy(
            source, target, send_sem, recv_sem, device_id=device, device_id_type=MESH
        ).start()

    def chain(step):
        for offset in (HOP, -HOP):
            target = {"tiles": along(offset) * SIDE + lane_x}
            pl.when(both_late(offset))(lambda: signal(chain_sem.at[step], target))

    def chain_wait(step):
        links = sum(jnp.where(both_late(offset), 1, 0) for offset in (HOP, -HOP))
        pl.when(late)(lambda: pl.semaphore_wait(chain_sem.at[step], links))

    chain(0)
    for offset in close:
        pl.when(below(offset))(lambda: signal(there_sem.at[-offset % planes], at_plane(offset)))
    for target in beside:
        copy(near.at[position], near.at[position], near_sem.at[0], near_sem.at[1], target)
    copy(tiles_hbm, tiles.at[mine], tile_sem.at[0], tile_sem.at[1], beside[0])

    spare = height_two + height_three
    table[spare:, :] = jnp.zeros((table.shape[0] - spare, half), BF16)
    chain_wait(0)
    chain(1)
    wait_bytes(near.at[pl.ds(0, len(beside))], near_sem.at[1])
    asked[pl.ds(plane, 1)] = jnp.sum(near[...], axis=0, keepdims=True)

    def pass_on(origin, offset, away):
        entry = asked.at[pl.ds(origin, 1)]
        copy(entry, entry, asked_sem.at[planes], asked_sem.at[away % planes], at_plane(offset))

    def arrival(away):
        wait_bytes(asked.at[pl.ds(along(-away), 1)], asked_sem.at[away % planes])

    for offset in close:
        pl.when(jnp.logical_or(late, below(offset)))(lambda: pass_on(plane, offset, offset))
    for offset in sorted(close, key=lambda offset: offset % planes if offset > 0 else planes - offset):
        @pl.when(above(offset))
        def _():
            pl.semaphore_wait(there_sem.at[offset % planes], 1)
            pass_on(plane, offset, offset)

    def to_early(offset):
        return along(offset) < split

    def soon(offset):
        sure = jnp.logical_and(to_early(offset), plane < planes - HOP)
        if offset == split - 1:
            sure = jnp.logical_and(sure, plane != split + 1)
        return sure

    def ask_distant(when):
        for offset in distant:
            pl.when(jnp.logical_and(late, when(offset)))(lambda: pass_on(plane, offset, offset))

    ask_distant(soon)
    chain_wait(1)
    chain(2)
    ask_distant(
        lambda offset: jnp.logical_and(
            jnp.logical_not(soon(offset)),
            to_early(offset) if abs(offset) > 3 * HOP else True,
        )
    )
    chain_wait(2)
    ask_distant(
        lambda offset: jnp.logical_not(to_early(offset)) if abs(offset) > 3 * HOP else False
    )

    ahead = jnp.logical_and(plane >= REACH, plane < planes - REACH)
    behind = jnp.logical_not(ahead)

    @pl.when(ahead)
    def _():
        arrival(REACH)

        @pl.when(along(-REACH) < split)
        def _():
            for step in range(1, AHEAD + 1):
                pass_on(along(-REACH), step, REACH + step)

    @pl.when(behind)
    def _():
        arrival(-REACH)

        @pl.when(along(REACH) < split)
        def _():
            for step in range(1, 2 * (split - REACH) - AHEAD):
                pass_on(along(REACH), -step, -REACH - step)

    for load in loads[5:]:
        load.wait()
    rows = SIDE * slab

    def select(origins):
        total = rows * len(origins)
        given = jnp.concatenate(
            [jnp.broadcast_to(asked[origin], (rows, LANES)) for origin in origins], axis=0
        )
        place = iota((total, LANES), 0) % rows
        kind = place % slab // together
        spot = kind * SIDE * together + place // slab * together + place % together
        lane = iota((total, LANES), 1)
        wanted = jnp.sum(jnp.where(lane == spot, given, 0), axis=1, keepdims=True)
        key = wanted + kind * height_two
        hot = jnp.concatenate(
            [one_hot(key == lane + start) for start in range(0, table.shape[0], LANES)], axis=1
        )
        picked = jnp.dot(hot, table[...], preferred_element_type=F32).astype(BF16)
        for index, origin in enumerate(origins):
            for c in range(chunks):
                send[c, pl.ds(origin * SIDE, SIDE)] = picked[
                    index * rows : (index + 1) * rows, c * LANES : (c + 1) * LANES
                ].reshape(SIDE, slab, LANES)

    def give(c, origin, others=(2, 1, 3, 0)):
        for step in others:
            other = origin * SIDE + lax.rem(lane_x + step, SIDE)
            copy(
                send.at[c, other], recv.at[c, me], rows_sem.at[0, c], rows_sem.at[1, c],
                {"tiles": other},
            )

    def serve(origin, away, parts):
        known = jnp.logical_or(
            jnp.logical_and(ahead, away == REACH),
            jnp.logical_and(behind, away == planes - REACH),
        )

        @pl.when(jnp.logical_not(known))
        def _():
            wait_bytes(asked.at[pl.ds(origin, 1)], asked_sem.at[away])

        select([origin])
        for c in parts:
            give(c, origin)

    select([plane])
    for c in range(chunks):
        recv[c, pl.ds(me, 1)] = send[c, pl.ds(me, 1)]
        give(c, plane, (2, 1, 3))
    for origin in range(FIRST):
        away = lax.rem(plane + planes - origin, planes)

        @pl.when(plane != origin)
        def _():
            serve(origin, away, range(chunks))

    def others(offsets, visit):
        for offset in offsets:
            origin = along(-offset)

            @pl.when(origin >= FIRST)
            def _():
                visit(origin, offset % planes)

    near_first = list(reversed(close))
    far_first = distant
    others(near_first, lambda origin, away: serve(origin, away, (0,)))
    others(reversed(distant), lambda origin, away: serve(origin, away, (0,)))
    others(far_first, lambda origin, away: give(1, origin))
    others(close, lambda origin, away: give(1, origin))

    wait_bytes(near.at[pl.ds(0, len(beside))], near_sem.at[0])
    wait_bytes(asked.at[pl.ds(0, 2 * REACH)], asked_sem.at[planes])

    @pl.when(late)
    def _():
        wait_bytes(asked.at[pl.ds(0, planes - 1 - 2 * REACH)], asked_sem.at[planes])

    @pl.when(jnp.logical_and(ahead, along(-REACH) < split))
    def _():
        wait_bytes(asked.at[pl.ds(0, AHEAD)], asked_sem.at[planes])

    @pl.when(jnp.logical_and(behind, along(REACH) < split))
    def _():
        wait_bytes(asked.at[pl.ds(0, 2 * (split - REACH) - AHEAD - 1)], asked_sem.at[planes])

    wait_bytes(tiles.at[pl.ds(0, count)], tile_sem.at[1])
    wait_bytes(tiles.at[pl.ds(0, count)], tile_sem.at[0])

    some = pl.ds(0, peers - 1)
    step = STEP
    depth = flat // peers
    summary = asked[plane]
    homes = []
    for which in range(together):
        spot = 2 * SIDE * together + lane_x * together + which
        homes.append(jnp.sum(jnp.where(lane == spot, summary, 0), axis=1, keepdims=True))
    for c in range(chunks):
        wait_bytes(recv.at[c, some], rows_sem.at[1, c])
        arranged[...] = jnp.dot(
            order[...], recv[c].reshape(wide, LANES), preferred_element_type=F32
        ).astype(BF16)
        terms = []
        for pair in range(0, together, 2):
            both = (pair, pair + 1)
            term = jnp.zeros((2 * inner, 2 * LANES), F32)
            for first in range(0, peers, step):
                product = jnp.concatenate(
                    [
                        jnp.concatenate(
                            [
                                arranged[(together + which) * peers : (together + which + 1) * peers, :]
                                * arranged[which * peers + j : which * peers + j + 1, :]
                                for which in both
                            ],
                            axis=1,
                        )
                        for j in range(first, first + step)
                    ],
                    axis=0,
                )
                left = jnp.concatenate(
                    [tiles[which, :, first * depth : (first + step) * depth] for which in both],
                    axis=0,
                )
                term = term + jnp.dot(left, product, preferred_element_type=F32)
            terms += [term[:inner, :LANES], term[inner:, LANES:]]
        def partial(group):
            total = jnp.zeros((inner, LANES), F32)
            for which in range(together):
                total = total + jnp.where(homes[which] == group, terms[which], 0.0)
            return total.astype(BF16)

        for other in owners:
            send_part[c, pl.ds(other, 1)] = partial(other).reshape(1, inner, LANES)
            copy(
                send_part.at[c, other], recv_part.at[c, row], part_sem.at[0, c],
                part_sem.at[1, c], {"blk": other},
            )
        recv_part[c, pl.ds(row, 1)] = partial(row).reshape(1, inner, LANES)
    for c in range(chunks):
        wait_bytes(recv_part.at[c, pl.ds(0, groups - 1)], part_sem.at[1, c])
        for side in range(CORES):
            total = recv_part[c, side].astype(F32)
            for group in range(side + CORES, groups, CORES):
                total = total + recv_part[c, group].astype(F32)
            start = side * half + c * LANES
            out_ref[:, start : start + LANES] = total
    for c in range(chunks):
        wait_bytes(send.at[c, some], rows_sem.at[0, c])
        wait_bytes(send_part.at[c, pl.ds(0, groups - 1)], part_sem.at[0, c])


def per_device(
    tensor_tiles, tile_iblock, tile_jslot, tile_kslot, block_jlist, block_klist, factor_b, factor_c
):
    groups = lax.axis_size("blk")
    peers = lax.axis_size("tiles")
    tiles = tensor_tiles[0]
    two = factor_b.reshape(factor_b.shape[0], factor_b.shape[2])
    three = factor_c.reshape(factor_c.shape[0], factor_c.shape[2])
    count, inner, flat = tiles.shape
    together = CORES * count
    rank = two.shape[1]
    half = rank // CORES
    chunks = half // LANES
    slab = 2 * together
    wide = peers * slab
    planes = peers // SIDE
    height = -(-(two.shape[0] + three.shape[0]) // LANES) * LANES
    dma = pltpu.SemaphoreType.DMA
    exchanged = pltpu.VMEM((chunks, peers, slab, LANES), BF16)
    part = pltpu.VMEM((chunks, groups, inner, LANES), BF16)
    return pl.pallas_call(
        functools.partial(kernel, groups, peers),
        out_shape=pltpu.VMEM((inner, rank), F32),
        in_specs=[pl.BlockSpec(memory_space=pl.ANY)] * 8,
        out_specs=pl.BlockSpec(memory_space=pltpu.VMEM),
        scratch_shapes=[
            *[pltpu.SMEM((1, count), jnp.int32)] * 5,
            pltpu.VMEM((together, inner, flat), BF16),
            pltpu.VMEM((height, half), BF16),
            pltpu.VMEM((SIDE * CORES, 1, LANES), jnp.int32),
            pltpu.VMEM((planes, 1, LANES), jnp.int32),
            pltpu.VMEM((wide, wide), BF16),
            exchanged, exchanged, pltpu.VMEM((wide, LANES), BF16), part, part,
            dma((8,)), dma((2,)), dma((2,)), dma((planes + 1,)), dma((2, chunks)), dma((2, chunks)),
            pltpu.SemaphoreType.REGULAR((planes,)), pltpu.SemaphoreType.REGULAR((3,)),
        ],
        compiler_params=pltpu.CompilerParams(collective_id=0, has_side_effects=True),
    )(tiles, tile_iblock, tile_jslot, tile_kslot, block_jlist, block_klist, two, three)


def solution(mesh):
    placed = (
        P("blk", "tiles", None, None),
        P("blk", "tiles"),
        P("blk", "tiles"),
        P("blk", "tiles"),
        P("blk", "tiles"),
        P("blk", "tiles"),
        P(None, "tiles", None),
        P(None, "tiles", None),
    )
    return jax.shard_map(
        per_device, mesh=mesh, in_specs=placed, out_specs=P(("blk", "tiles"), None), check_vma=False
    )
```
